1024 devices in a mesh: elem: 128 (over y, z), lev: 8 (over x, core).
Axes of the slice: x: 4, y: 8, z: 16, core: 2. Of those that a mesh axis runs over, the one named last changes fastest.
Arguments:
- tracers: bfloat16 [16384, 32, 1024], P('elem', 'lev'), may hold values from -6 to 6
- velocity: float32 [3, 16, 32, 16384], P(None, None, 'lev', 'elem'), may hold values from -6 to 6
- node_mass: float32 [16, 16384], P(None, 'elem'), may hold values from 0.5 to 2
- source: int32 [16384], P('elem'), may hold values from 0 to 16383, as said below
Outputs:
- advected: bfloat16 [16384, 32, 1024], P('elem', 'lev')
The draws below stay inside these ranges and needn't reach their ends.
Inputs may be any that keep to these rules, and one draw needn't show every extreme that they name: The source of element e lies at most 64 elements before or after e along the curve, cyclically over 16384 elements. Within each aligned run of 128 elements, only the first 32 may take a source before the run and only the last 32 one after it; in every draw some run has all of its first 32 elements taking sources 64 elements before them, and some run all of its last 32 elements taking sources 64 elements after them.
All inputs are finite; a program needn't handle non-finite values.
Results may differ from the reference program's by a relative error of at most 0.006.
Values may be sent and summed in bfloat16 or wider, within the bound.
A program may use at most 32 MiB of HBM per device.

```python
import math
import jax
import jax.numpy as jnp
import numpy as np
from jax import lax

NODES = 16
Q = 64
E_DEV = 128
SPAN = 64
CAP = 32
ELEMS = 16384
LEVELS = 32


def draw_source(key, part):
    first_key, second_key, third_key = jax.random.split(jax.random.fold_in(key, 7301), 3)
    element = jnp.arange(ELEMS, dtype=jnp.int32)
    position = element % E_DEV
    backward = E_DEV - 1 - position
    lowest = jnp.where(position < CAP, -SPAN, jnp.maximum(-SPAN, -position))
    highest = jnp.where(backward < CAP, SPAN, jnp.minimum(SPAN, backward))
    raw_draw = jax.random.randint(first_key, (ELEMS,), 0, 1 << 20, dtype=jnp.int32)
    offset = lowest + raw_draw % (highest - lowest + 1)
    run_index = element // E_DEV
    chosen_before = jax.random.randint(second_key, (), 0, ELEMS // E_DEV, dtype=jnp.int32)
    chosen_after = jax.random.randint(third_key, (), 0, ELEMS // E_DEV, dtype=jnp.int32)
    offset = jnp.where((run_index == chosen_before) & (position < CAP), -SPAN, offset)
    offset = jnp.where((run_index == chosen_after) & (backward < CAP), SPAN, offset)
    return ((element + offset) % ELEMS).astype(jnp.int32)


def block_scale(stream_key, extent, cuts, low, top_value):
    level = 1.0
    for dim, parts in cuts:
        steps = jax.random.uniform(jax.random.fold_in(jax.random.fold_in(stream_key, 6), dim), (parts,), jnp.float32, low / len(cuts), top_value / len(cuts))
        level = level * jnp.repeat(jnp.exp(steps), extent[dim] // parts).reshape((-1,) + (1,) * (len(extent) - 1 - dim))
    return level


def gaussian(key, dims, width, reach, shards=(), held_as=jnp.bfloat16):
    gain = block_scale(key, dims, shards, -0.22, 0.18) if shards else 1.0
    values = jax.random.normal(key, dims, jnp.float32) * width * gain
    return jnp.minimum(jnp.maximum(values, -reach), reach).astype(held_as)


def setup_inputs(seed: int = 0) -> dict:
    keys = jax.random.split(jax.random.key(seed), 5)
    tracers = gaussian(keys[0], (ELEMS, LEVELS, NODES * Q), 1.0, 6.0, ((0, 128), (1, 8)))
    velocity = gaussian(keys[1], (3, NODES, LEVELS, ELEMS), 1.0, 6.0, ((2, 8), (3, 128)), jnp.float32)
    node_mass = jnp.clip(jnp.exp(math.log(2.0) - 1.3862944 * jax.random.uniform(keys[2], (NODES, ELEMS), jnp.float32) ** block_scale(keys[2], (NODES, ELEMS), ((1, 128),), -0.2, 0.2)), 0.5, 2.0)
    source = draw_source(jax.random.fold_in(keys[4], 71), 0)
    return {"tracers": tracers, "velocity": velocity, "node_mass": node_mass, "source": source}


gll_points = (-1.0, -0.4472135954999579, 0.4472135954999579, 1.0)
east_nodes = np.array([3, 7, 11, 15])
west_nodes = np.array([0, 4, 8, 12])
courant = 0.15


def lagrange(position):
    columns = []
    for column in range(4):
        factor = jnp.ones_like(position)
        for other in range(4):
            if other != column:
                factor = factor * (position - gll_points[other]) / (gll_points[column] - gll_points[other])
        columns.append(factor)
    return jnp.stack(columns, axis=-1)


def weights(horizontal):
    along_nodes = jnp.array([gll_points[node % 4] for node in range(16)], jnp.float32)
    across_nodes = jnp.array([gll_points[node // 4] for node in range(16)], jnp.float32)
    along_basis = lagrange(along_nodes - courant * horizontal[..., 0])
    across_basis = lagrange(across_nodes - courant * horizontal[..., 1])
    table = across_basis[..., :, :, None] * along_basis[..., :, None, :]
    return table.reshape(table.shape[:-2] + (16,)).astype(jnp.bfloat16)


def share_edges(field, node_mass):
    east = field[:, east_nodes, :]
    west = field[:, west_nodes, :]
    mass_east = node_mass[:, east_nodes][:, :, None]
    mass_west = node_mass[:, west_nodes][:, :, None]
    west_after = jnp.roll(west, -1, axis=0)
    mass_after = jnp.roll(mass_west, -1, axis=0)
    shared = (mass_east * east + mass_after * west_after) / (mass_east + mass_after)
    field = field.at[:, east_nodes, :].set(shared)
    return field.at[:, west_nodes, :].set(jnp.roll(shared, 1, axis=0))


def reference(tracers, velocity, node_mass, source):
    elements, levels_all, columns_all = tracers.shape
    tracer_count = columns_all // 16
    winds_all = jnp.transpose(velocity, (3, 2, 0, 1))
    masses = jnp.transpose(node_mass)

    def one_level(level):
        here = lax.dynamic_index_in_dim(tracers, level, 1, keepdims=False).astype(jnp.float32)
        upper = lax.dynamic_index_in_dim(tracers, jnp.maximum(level - 1, 0), 1, keepdims=False).astype(jnp.float32)
        upper = jnp.where(level > 0, upper, jnp.zeros((), jnp.float32))
        winds = lax.dynamic_index_in_dim(winds_all, level, 1, keepdims=False)
        descent = jax.nn.sigmoid(winds[:, 2, :])[:, :, None]
        lifted = ((1.0 - descent) * here.reshape(elements, 16, tracer_count)
                  + descent * upper.reshape(elements, 16, tracer_count)).astype(jnp.bfloat16)
        horizontal = share_edges(jnp.swapaxes(winds[:, :2, :], 1, 2), masses)
        table = weights(horizontal)
        blocks = jnp.take(lifted, source, axis=0)
        moved = jnp.einsum("enm,emt->ent", table.astype(jnp.float32), blocks.astype(jnp.float32),
                           precision=lax.Precision.HIGHEST).astype(jnp.bfloat16)
        final = share_edges(moved.astype(jnp.float32), masses).astype(jnp.bfloat16)
        return final.reshape(elements, columns_all)

    stacked = lax.map(one_level, jnp.arange(levels_all, dtype=jnp.int32))
    return jnp.swapaxes(stacked, 0, 1)
```

```python
import functools

import jax
import jax.numpy as jnp
from jax import lax
from jax.experimental import pallas as pl
from jax.experimental.pallas import tpu as pltpu
from jax.sharding import PartitionSpec as P

MESH = pl.DeviceIdType.MESH
gll = (-1.0, -0.4472135954999579, 0.4472135954999579, 1.0)
courant = 0.15
f32 = jnp.float32
bf16 = jnp.bfloat16
CH = 4
TQ = 64 // CH


def dot(a, b):
    return lax.dot_general(a, b, (((1,), (0,)), ((), ())), preferred_element_type=f32)


def dot_t(a, b):
    return lax.dot_general(a, b, (((1,), (1,)), ((), ())), preferred_element_type=f32)


def dot_exact(a, b):
    return lax.dot_general(
        a, b, (((1,), (0,)), ((), ())), preferred_element_type=f32, precision=lax.Precision.HIGHEST
    )


def iota(shape, dim):
    return lax.broadcasted_iota(jnp.int32, shape, dim)


def one_hot(rows, code):
    return jnp.where(iota((rows, code.shape[1]), 0) == code, 1.0, 0.0).astype(bf16)


def basis(x):
    out = []
    for a in range(4):
        others = [b for b in range(4) if b != a]
        scale = 1.0
        for b in others:
            scale = scale / (gll[a] - gll[b])
        f = (x - gll[others[0]]) * (x - gll[others[1]]) * (x - gll[others[2]]) * scale
        out.append(f)
    return out


def kernel(
    peers_elem, peers_lev, total,
    t_ref, v_ref, mass_ref, src_ref, o_ref,
    tt, wind, massx, msg_to_next, msg_to_prev, msg_prev, msg_next,
    x3_send, x3_recv, lifted, pack_next, pack_prev, halo_prev, halo_next,
    gath, wtab, moved, edge_to_next, edge_to_prev, edges,
    msg_sem, x3_sem, halo_sem, edge_sem,
):
    elem = lax.axis_index("elem")
    lev = lax.axis_index("lev")
    nxt = lax.rem(elem + 1, peers_elem)
    prv = lax.rem(elem + peers_elem - 1, peers_elem)
    below = lax.rem(lev + 1, peers_lev)
    above = lax.rem(lev + peers_lev - 1, peers_lev)

    barrier = pltpu.get_barrier_semaphore()
    for target in ({"elem": nxt}, {"elem": prv}, {"lev": below}, {"lev": above}):
        pl.semaphore_signal(barrier, inc=1, device_id=target, device_id_type=MESH)

    def remote(src, dst, sems, target):
        return pltpu.make_async_remote_copy(
            src_ref=src, dst_ref=dst, send_sem=sems.at[0], recv_sem=sems.at[1],
            device_id=target, device_id_type=MESH,
        )

    lane = iota((1, 128), 1)
    level = jnp.bitwise_and(lane, 3)
    wide_lane = iota((128, 512), 1)
    wide_row = iota((128, 512), 0)

    mass_all = mass_ref[...]
    start = elem * 128
    rel = src_ref[...] - start + 64
    rel = jnp.where(rel < 0, rel + total, rel)
    rel = jnp.where(rel >= total, rel - total, rel)
    rel8 = jnp.broadcast_to(rel.astype(f32), (8, 128))
    spread_all = jnp.where(wide_row == jnp.right_shift(wide_lane, 2), 1.0, 0.0)
    mass_wide = dot_exact(mass_all, spread_all)
    rel_wide = dot_exact(rel8, spread_all)
    acc = None
    for k in range(4):
        spread = jnp.where(wide_row * 4 + k == wide_lane, 1.0, 0.0)
        rows = jnp.concatenate([v_ref[comp, :, k, :] for comp in range(3)], axis=0)
        part = dot_exact(rows, spread)
        acc = part if acc is None else acc + part

    def col(c):
        return slice(128 * c, 128 * (c + 1))

    for c in range(4):
        wind[c] = acc[:, col(c)]
        massx[c, 0:16, :] = mass_wide[:, col(c)]
        massx[c, 16:24, :] = rel_wide[:, col(c)]

    def side(ref, base, first, c):
        return ref[c, pl.ds(base + first, 4, stride=4), :]

    for message, first, c in ((msg_to_next, 3, 3), (msg_to_prev, 0, 0)):
        message[0:4, :] = side(wind, 0, first, c)
        message[4:8, :] = side(wind, 16, first, c)
        message[8:12, :] = side(massx, 0, first, c)
        message[12:16, :] = side(massx, 0, first, c)
        message[16:24, :] = massx[c, 16:24, :]

    pl.semaphore_wait(barrier, 4)
    send_a = remote(msg_to_next, msg_prev, msg_sem.at[0], {"elem": nxt})
    send_b = remote(msg_to_prev, msg_next, msg_sem.at[1], {"elem": prv})
    send_a.start()
    send_b.start()

    eye = jnp.where(iota((128, 128), 0) == iota((128, 128), 1), 1.0, 0.0).astype(bf16)
    for block in range(8):
        turned = dot_t(eye, t_ref[:, 128 * block : 128 * (block + 1)])
        tt[2 * block : 2 * block + 2, :, :] = turned.astype(bf16).reshape(2, 64, 512)

    pick = jnp.where(iota((512, 128), 0) == iota((512, 128), 1) * 4 + 3, 1.0, 0.0).astype(bf16)

    def x3_copy(q):
        return remote(x3_send.at[q], x3_recv.at[q], x3_sem.at[q], {"lev": below})

    def send_x3(q, carry):
        chunk = tt[:, pl.ds(pl.multiple_of(q * TQ, TQ), TQ), :].reshape(16 * TQ, 512)
        x3_send[q] = dot(chunk, pick).astype(bf16)
        x3_copy(q).start()
        return carry

    lax.fori_loop(0, CH, send_x3, 0)

    send_a.wait()
    send_b.wait()

    def pair(ref, first, c, rows):
        return jnp.concatenate([side(ref, base, first, c) for base in rows], axis=0)

    def after(a, b):
        return jnp.where(lane < 124, pltpu.roll(a, 124, 1), pltpu.roll(b, 124, 1))

    def before(a, b):
        return jnp.where(lane < 4, pltpu.roll(a, 4, 1), pltpu.roll(b, 4, 1))

    wind_east = [msg_prev[0:8, :]] + [pair(wind, 3, c, (0, 16)) for c in range(4)]
    wind_west = [pair(wind, 0, c, (0, 16)) for c in range(4)] + [msg_next[0:8, :]]
    mass_east = [msg_prev[8:16, :]] + [pair(massx, 3, c, (0, 0)) for c in range(4)]
    mass_west = [pair(massx, 0, c, (0, 0)) for c in range(4)] + [msg_next[8:16, :]]
    west_now = [wind_west[0]] + wind_west[:4]
    mass_now = [mass_west[0]] + mass_west[:4]
    part_east, part_west, shared = [], [], []
    for i in range(5):
        mass_next = after(mass_now[i], mass_west[i])
        wind_next = after(west_now[i], wind_west[i])
        inverse = 1.0 / (mass_east[i] + mass_next)
        part_east.append(mass_east[i] * inverse)
        part_west.append(mass_next * inverse)
        shared.append((mass_east[i] * wind_east[i] + mass_next * wind_next) * inverse)
    for c in range(4):
        new_west = before(shared[c], shared[c + 1])
        for comp in range(2):
            wind[c, pl.ds(16 * comp + 3, 4, stride=4), :] = shared[c + 1][4 * comp : 4 * comp + 4]
            wind[c, pl.ds(16 * comp, 4, stride=4), :] = new_west[4 * comp : 4 * comp + 4]

    node = iota((16, 1), 0)

    def point(i):
        out = jnp.full((16, 1), gll[3], f32)
        for a in range(3):
            out = jnp.where(i == a, gll[a], out)
        return out

    along_point = point(jnp.bitwise_and(node, 3))
    across_point = point(jnp.right_shift(node, 2))
    for c in range(4):
        along = basis(along_point - courant * wind[c, 0:16, :])
        across = basis(across_point - courant * wind[c, 16:32, :])
        for m in range(16):
            product = across[m // 4] * along[m % 4]
            wtab[c, 16 * m : 16 * m + 16, :] = product.astype(bf16).astype(f32)

    for c in range(4):
        wind[c, 32:48, :] = 1.0 / (1.0 + jnp.exp(-wind[c, 32:48, :]))

    def code(row, shift):
        return (row.astype(jnp.int32) + shift) * 4 + level

    ask_next = one_hot(256, code(msg_next[16:17, :], 0))
    ask_prev = one_hot(256, code(msg_prev[16:17, :], -192))
    pick_here = [one_hot(512, code(massx[c, 16:17, :], -64)) for c in range(4)]
    step_down = jnp.where(
        (iota((128, 128), 0) + 1 == iota((128, 128), 1)) & (level != 0), 1.0, 0.0
    ).astype(bf16)
    has_above = jnp.where(lev > 0, 1.0, 0.0)
    enter = [
        (jnp.where((iota((128, 128), 0) * 4 - 128 * c) == iota((128, 128), 1), 1.0, 0.0) * has_above).astype(bf16)
        for c in range(4)
    ]

    def halo_copies(q):
        return (
            remote(pack_next.at[q], halo_prev.at[q], halo_sem.at[q, 0], {"elem": nxt}),
            remote(pack_prev.at[q], halo_next.at[q], halo_sem.at[q, 1], {"elem": prv}),
        )

    def lift(q, carry):
        rows = pl.ds(pl.multiple_of(q * TQ, TQ), TQ)
        x3_copy(q).wait()
        extra = x3_recv[q]
        for c in range(4):
            here = tt[:, rows, col(c)].reshape(16 * TQ, 128)
            upper = dot(here, step_down) + dot(extra, enter[c])
            descent = jnp.broadcast_to(wind[c, 32:48, :][:, None, :], (16, TQ, 128)).reshape(16 * TQ, 128)
            value = (1.0 - descent) * here.astype(f32) + descent * upper
            lifted[q, :, col(c)] = value.astype(bf16)
        pack_next[q] = dot(lifted[q, :, 256:512], ask_next).astype(bf16)
        pack_prev[q] = dot(lifted[q, :, 0:256], ask_prev).astype(bf16)
        for copy in halo_copies(q):
            copy.start()
        return carry

    lax.fori_loop(0, CH, lift, 0)

    def gather(q, carry):
        for c in range(4):
            gath[q, c] = dot(lifted[q], pick_here[c]).astype(bf16)
        return carry

    lax.fori_loop(0, CH, gather, 0)

    def move(q, c, block):
        rows = pl.ds(pl.multiple_of(q * TQ, TQ), TQ)
        values = [block[TQ * m : TQ * (m + 1), :] for m in range(16)]
        for n in range(16):
            total_n = None
            for m in range(16):
                term = wtab[c, pl.ds(16 * m + n, 1), :] * values[m]
                total_n = term if total_n is None else total_n + term
            moved[c, n, rows, :] = total_n.astype(bf16)

    def inner(i, carry):
        q, c = i // 2, lax.rem(i, 2) + 1
        move(q, c, gath[q, c].astype(f32))
        return carry

    lax.fori_loop(0, 2 * CH, inner, 0)

    def outer(q, carry):
        for copy in halo_copies(q):
            copy.wait()
        move(q, 0, gath[q, 0].astype(f32) + halo_prev[q].astype(f32))
        move(q, 3, gath[q, 3].astype(f32) + halo_next[q].astype(f32))
        return carry

    lax.fori_loop(0, CH, outer, 0)

    east_end = jnp.concatenate([moved[3, 4 * j + 3] for j in range(4)], axis=0)
    west_end = jnp.concatenate([moved[0, 4 * j] for j in range(4)], axis=0)
    edge_to_next[...] = dot_t(eye[112:128], east_end).astype(bf16)
    edge_to_prev[...] = dot_t(eye[0:16], west_end).astype(bf16)
    edges[16:112, :] = jnp.zeros((96, 256), bf16)
    last_a = remote(edge_to_next, edges.at[112:128], edge_sem.at[0], {"elem": nxt})
    last_b = remote(edge_to_prev, edges.at[0:16], edge_sem.at[1], {"elem": prv})
    last_a.start()
    last_b.start()
    last_a.wait()
    last_b.wait()
    outside = jnp.transpose(edges[...].astype(f32))

    for j in range(4):
        mine = outside[64 * j : 64 * j + 64]
        east = [mine] + [moved[c, 4 * j + 3].astype(f32) for c in range(4)]
        west = [moved[c, 4 * j].astype(f32) for c in range(4)] + [mine]
        now = [west[0]] + west[:4]
        joint = []
        for i in range(5):
            joint.append(
                part_east[i][j : j + 1] * east[i] + part_west[i][j : j + 1] * after(now[i], west[i])
            )
        for c in range(4):
            moved[c, 4 * j + 3] = joint[c + 1].astype(bf16)
            moved[c, 4 * j] = before(joint[c], joint[c + 1]).astype(bf16)

    for c in range(4):
        o_ref[col(c), :] = dot_t(eye, moved[c].reshape(1024, 128)).astype(bf16)


def solution(mesh):
    peers_elem, peers_lev = mesh.shape["elem"], mesh.shape["lev"]

    def on_device(tracers, velocity, node_mass, source):
        elements, levels, columns = tracers.shape
        vmem = pl.BlockSpec(memory_space=pltpu.VMEM)
        out = pl.pallas_call(
            functools.partial(kernel, peers_elem, peers_lev, elements * peers_elem),
            out_shape=jax.ShapeDtypeStruct((elements * levels, columns), bf16),
            in_specs=[vmem] * 4,
            out_specs=vmem,
            scratch_shapes=[
                pltpu.VMEM((16, 64, 512), bf16),
                pltpu.VMEM((4, 48, 128), f32),
                pltpu.VMEM((4, 24, 128), f32),
                pltpu.VMEM((24, 128), f32),
                pltpu.VMEM((24, 128), f32),
                pltpu.VMEM((24, 128), f32),
                pltpu.VMEM((24, 128), f32),
                pltpu.VMEM((CH, 16 * TQ, 128), bf16),
                pltpu.VMEM((CH, 16 * TQ, 128), bf16),
                pltpu.VMEM((CH, 16 * TQ, 512), bf16),
                pltpu.VMEM((CH, 16 * TQ, 128), bf16),
                pltpu.VMEM((CH, 16 * TQ, 128), bf16),
                pltpu.VMEM((CH, 16 * TQ, 128), bf16),
                pltpu.VMEM((CH, 16 * TQ, 128), bf16),
                pltpu.VMEM((CH, 4, 16 * TQ, 128), bf16),
                pltpu.VMEM((4, 256, 128), f32),
                pltpu.VMEM((4, 16, 64, 128), bf16),
                pltpu.VMEM((16, 256), bf16),
                pltpu.VMEM((16, 256), bf16),
                pltpu.VMEM((128, 256), bf16),
                pltpu.SemaphoreType.DMA((2, 2)),
                pltpu.SemaphoreType.DMA((CH, 2)),
                pltpu.SemaphoreType.DMA((CH, 2, 2)),
                pltpu.SemaphoreType.DMA((2, 2)),
            ],
            compiler_params=pltpu.CompilerParams(collective_id=0, has_side_effects=True),
            name="transport",
        )(
            tracers.reshape(elements * levels, columns),
            velocity,
            node_mass,
            source.reshape(1, elements),
        )
        return out.reshape(elements, levels, columns)

    placed = (P("elem", "lev", None), P(None, None, "lev", "elem"), P(None, "elem"), P("elem"))
    return jax.shard_map(
        on_device, mesh=mesh, in_specs=placed, out_specs=P("elem", "lev", None), check_vma=False
    )
```

```python
import functools

import jax
import jax.numpy as jnp
from jax import lax
from jax.experimental import pallas as pl
from jax.experimental.pallas import tpu as pltpu
from jax.sharding import PartitionSpec as P

MESH = pl.DeviceIdType.MESH
gll = (-1.0, -0.4472135954999579, 0.4472135954999579, 1.0)
courant = 0.15
f32 = jnp.float32
bf16 = jnp.bfloat16
CH = 4
TQ = 64 // CH


def dot(a, b):
    return lax.dot_general(a, b, (((1,), (0,)), ((), ())), preferred_element_type=f32)


def dot_t(a, b):
    return lax.dot_general(a, b, (((1,), (1,)), ((), ())), preferred_element_type=f32)


def three(x):
    top = x.astype(bf16)
    rest = x - top.astype(f32)
    middle = rest.astype(bf16)
    low = (rest - middle.astype(f32)).astype(bf16)
    return [top, middle, low]


def iota(shape, dim):
    return lax.broadcasted_iota(jnp.int32, shape, dim)


def one_hot(rows, code):
    return jnp.where(iota((rows, code.shape[1]), 0) == code, 1.0, 0.0).astype(bf16)


def basis(x):
    out = []
    for a in range(4):
        others = [b for b in range(4) if b != a]
        scale = 1.0
        for b in others:
            scale = scale / (gll[a] - gll[b])
        f = (x - gll[others[0]]) * (x - gll[others[1]]) * (x - gll[others[2]]) * scale
        out.append(f)
    return out


def kernel(
    peers_elem, peers_lev, total,
    t_hbm, v_hbm, mass_hbm, src_hbm, o_hbm,
    t_ref, v_ref, mass_ref, src_ref, out,
    tt, wind, massx, msg_to_next, msg_to_prev, msg_prev, msg_next,
    x3_send, x3_recv, lifted, pack_next, pack_prev, halo_prev, halo_next,
    gath, wtab, moved, edge_to_next, edge_to_prev, edges,
    enter, ask, pick_here, parts, late_west, late_east,
    in_sem, out_sem, msg_sem, x3_sem, halo_sem, edge_sem,
):
    elem = lax.axis_index("elem")
    lev = lax.axis_index("lev")
    nxt = lax.rem(elem + 1, peers_elem)
    prv = lax.rem(elem + peers_elem - 1, peers_elem)
    below = lax.rem(lev + 1, peers_lev)
    above = lax.rem(lev + peers_lev - 1, peers_lev)

    barrier = pltpu.get_barrier_semaphore()
    for target in ({"elem": nxt}, {"elem": prv}, {"lev": below}, {"lev": above}):
        pl.semaphore_signal(barrier, inc=1, device_id=target, device_id_type=MESH)

    def arrive(i, src, dst):
        copy = pltpu.make_async_copy(src, dst, in_sem.at[i])
        copy.start()
        return copy

    small = [arrive(1, v_hbm, v_ref), arrive(2, mass_hbm, mass_ref), arrive(3, src_hbm, src_ref)]
    large = arrive(0, t_hbm, t_ref)

    def remote(src, dst, sems, target):
        return pltpu.make_async_remote_copy(
            src_ref=src, dst_ref=dst, send_sem=sems.at[0], recv_sem=sems.at[1],
            device_id=target, device_id_type=MESH,
        )

    lane = iota((1, 128), 1)
    level = jnp.bitwise_and(lane, 3)

    def col(c):
        return slice(128 * c, 128 * (c + 1))

    for copy in small:
        copy.wait()
    rel = src_ref[...] - elem * 128 + 64
    rel = jnp.where(rel < 0, rel + total, rel)
    rel = jnp.where(rel >= total, rel - total, rel)
    rel16 = jnp.broadcast_to(rel.astype(f32), (16, 128)).astype(bf16)
    wide_lane = iota((128, 512), 1)
    wide_row = iota((128, 512), 0)
    spread_all = jnp.where(wide_row == jnp.right_shift(wide_lane, 2), 1.0, 0.0).astype(bf16)
    slow = dot(jnp.concatenate(three(mass_ref[...]) + [rel16], axis=0), spread_all)
    mass_wide = slow[0:16] + slow[16:32] + slow[32:48]
    rel_wide = slow[48:56]
    rows = jnp.concatenate(
        [
            jnp.concatenate([v_ref[comp, :, k, :] for comp in range(3)], axis=0)
            for k in range(4)
        ],
        axis=1,
    )
    spread = jnp.concatenate(
        [jnp.where(wide_row * 4 + k == wide_lane, 1.0, 0.0).astype(bf16) for k in range(4)], axis=0
    )
    fast = dot(jnp.concatenate(three(rows), axis=0), spread)
    fast = fast[0:48] + fast[48:96] + fast[96:144]
    for c in range(4):
        wind[c] = fast[:, col(c)]
        massx[c, 0:16, :] = mass_wide[:, col(c)]
        massx[c, 16:24, :] = rel_wide[:, col(c)]

    def side(ref, base, first, c):
        return ref[c, pl.ds(base + first, 4, stride=4), :]

    for message, first, c in ((msg_to_next, 3, 3), (msg_to_prev, 0, 0)):
        message[0:4, :] = side(wind, 0, first, c)
        message[4:8, :] = side(wind, 16, first, c)
        message[8:12, :] = side(massx, 0, first, c)
        message[12:16, :] = side(massx, 0, first, c)
        message[16:24, :] = massx[c, 16:24, :]

    large.wait()
    for block in range(8):
        turned = t_ref[:, :, 128 * block : 128 * (block + 1)].reshape(512, 128).T
        tt[2 * block : 2 * block + 2, :, :] = turned.reshape(2, 64, 512)

    pick = jnp.where(iota((512, 128), 0) == iota((512, 128), 1) * 4 + 3, 1.0, 0.0).astype(bf16)

    def x3_copy(q):
        return remote(x3_send.at[q], x3_recv.at[q], x3_sem.at[q], {"lev": below})

    def make_x3(q):
        chunk = tt[:, TQ * q : TQ * (q + 1), :].reshape(16 * TQ, 512)
        x3_send[q] = dot(chunk, pick).astype(bf16)

    for q in range(CH):
        make_x3(q)

    pl.semaphore_wait(barrier, 4)
    send_a = remote(msg_to_next, msg_prev, msg_sem.at[0], {"elem": nxt})
    send_b = remote(msg_to_prev, msg_next, msg_sem.at[1], {"elem": prv})
    send_a.start()
    send_b.start()
    for q in range(CH):
        x3_copy(q).start()

    for c in range(4):
        wind[c, 32:48, :] = 1.0 / (1.0 + jnp.exp(-wind[c, 32:48, :]))

    def code(row, shift):
        return (row.astype(jnp.int32) + shift) * 4 + level

    has_above = jnp.where(lev > 0, 1.0, 0.0)
    step_down = (iota((128, 128), 0) + 1 == iota((128, 128), 1)) & (level != 0)
    for c in range(4):
        enter[c, 0:128, :] = jnp.where(step_down, 1.0, 0.0).astype(bf16)
        entry = iota((128, 128), 0) * 4 - 128 * c == iota((128, 128), 1)
        enter[c, 128:256, :] = (jnp.where(entry, 1.0, 0.0) * has_above).astype(bf16)
    for i, pair in enumerate(((1, 2), (0, 3))):
        for side_of, c in enumerate(pair):
            pick_here[i, :, col(side_of)] = one_hot(512, code(massx[c, 16:17, :], -64))

    send_a.wait()
    send_b.wait()
    ask[0] = one_hot(256, code(msg_next[16:17, :], 0))
    ask[1] = one_hot(256, code(msg_prev[16:17, :], -192))

    def halo_copies(q):
        return (
            remote(pack_next.at[q], halo_prev.at[q], halo_sem.at[q, 0], {"elem": nxt}),
            remote(pack_prev.at[q], halo_next.at[q], halo_sem.at[q, 1], {"elem": prv}),
        )

    def lift(q, carry):
        rows = pl.ds(pl.multiple_of(q * TQ, TQ), TQ)
        x3_copy(q).wait()
        extra = x3_recv[q]
        for c in range(4):
            here = tt[:, rows, col(c)].reshape(16 * TQ, 128)
            upper = dot(jnp.concatenate([here, extra], axis=1), enter[c])
            descent = jnp.broadcast_to(wind[c, 32:48, :][:, None, :], (16, TQ, 128)).reshape(16 * TQ, 128)
            value = (1.0 - descent) * here.astype(f32) + descent * upper
            lifted[q, :, col(c)] = value.astype(bf16)
        pack_next[q] = dot(lifted[q, :, 256:512], ask[0]).astype(bf16)
        pack_prev[q] = dot(lifted[q, :, 0:256], ask[1]).astype(bf16)
        for copy in halo_copies(q):
            copy.start()
        return carry

    lax.fori_loop(0, CH, lift, 0)

    def pair(ref, first, c, rows):
        return jnp.concatenate([side(ref, base, first, c) for base in rows], axis=0)

    def after(a, b):
        return jnp.where(lane < 124, pltpu.roll(a, 124, 1), pltpu.roll(b, 124, 1))

    def before(a, b):
        return jnp.where(lane < 4, pltpu.roll(a, 4, 1), pltpu.roll(b, 4, 1))

    wind_east = [msg_prev[0:8, :]] + [pair(wind, 3, c, (0, 16)) for c in range(4)]
    wind_west = [pair(wind, 0, c, (0, 16)) for c in range(4)] + [msg_next[0:8, :]]
    mass_east = [msg_prev[8:16, :]] + [pair(massx, 3, c, (0, 0)) for c in range(4)]
    mass_west = [pair(massx, 0, c, (0, 0)) for c in range(4)] + [msg_next[8:16, :]]
    west_now = [wind_west[0]] + wind_west[:4]
    mass_now = [mass_west[0]] + mass_west[:4]
    shared = []
    for i in range(5):
        mass_next = after(mass_now[i], mass_west[i])
        wind_next = after(west_now[i], wind_west[i])
        inverse = 1.0 / (mass_east[i] + mass_next)
        parts[0, i] = mass_east[i] * inverse
        parts[1, i] = mass_next * inverse
        shared.append((mass_east[i] * wind_east[i] + mass_next * wind_next) * inverse)
    for c in range(4):
        new_west = before(shared[c], shared[c + 1])
        for comp in range(2):
            wind[c, pl.ds(16 * comp + 3, 4, stride=4), :] = shared[c + 1][4 * comp : 4 * comp + 4]
            wind[c, pl.ds(16 * comp, 4, stride=4), :] = new_west[4 * comp : 4 * comp + 4]

    node = iota((16, 1), 0)

    def point(i):
        value = jnp.full((16, 1), gll[3], f32)
        for a in range(3):
            value = jnp.where(i == a, gll[a], value)
        return value

    along_point = point(jnp.bitwise_and(node, 3))
    across_point = point(jnp.right_shift(node, 2))
    for c in range(4):
        along = basis(along_point - courant * wind[c, 0:16, :])
        across = basis(across_point - courant * wind[c, 16:32, :])
        for m in range(16):
            product = across[m // 4] * along[m % 4]
            wtab[c, 16 * m : 16 * m + 16, :] = product.astype(bf16).astype(f32)

    def gather(q, carry):
        for i, columns in enumerate(((1, 2), (0, 3))):
            block = dot(lifted[q], pick_here[i]).astype(bf16)
            for half, c in enumerate(columns):
                gath[q, c] = block[:, col(half)]
        return carry

    lax.fori_loop(0, CH, gather, 0)

    def move(q, c, block):
        rows = pl.ds(pl.multiple_of(q * TQ, TQ), TQ)
        values = [block[TQ * m : TQ * (m + 1), :] for m in range(16)]
        for n in range(16):
            total_n = None
            for m in range(16):
                term = wtab[c, pl.ds(16 * m + n, 1), :] * values[m]
                total_n = term if total_n is None else total_n + term
            moved[c, n, rows, :] = total_n.astype(bf16)

    def inner(i, carry):
        q, c = i // 2, lax.rem(i, 2) + 1
        move(q, c, gath[q, c].astype(f32))
        return carry

    lax.fori_loop(0, 2 * CH, inner, 0)

    def outer(q, carry):
        for copy in halo_copies(q):
            copy.wait()
        move(q, 0, gath[q, 0].astype(f32) + halo_prev[q].astype(f32))
        move(q, 3, gath[q, 3].astype(f32) + halo_next[q].astype(f32))
        return carry

    lax.fori_loop(0, CH, outer, 0)

    eye = jnp.where(iota((128, 128), 0) == iota((128, 128), 1), 1.0, 0.0).astype(bf16)
    east_end = jnp.concatenate([moved[3, 4 * j + 3] for j in range(4)], axis=0)
    west_end = jnp.concatenate([moved[0, 4 * j] for j in range(4)], axis=0)
    edge_to_next[...] = dot_t(eye[112:128], east_end).astype(bf16)
    edge_to_prev[...] = dot_t(eye[0:16], west_end).astype(bf16)
    last_a = remote(edge_to_next, edges.at[112:128], edge_sem.at[0], {"elem": nxt})
    last_b = remote(edge_to_prev, edges.at[0:16], edge_sem.at[1], {"elem": prv})
    last_a.start()
    last_b.start()
    edges[16:112, :] = jnp.zeros((96, 256), bf16)

    for j in range(4):
        east = [moved[c, 4 * j + 3].astype(f32) for c in range(4)]
        west = [moved[c, 4 * j].astype(f32) for c in range(4)]
        joint = []
        for c in range(3):
            joint.append(
                parts[0, c + 1, j : j + 1] * east[c]
                + parts[1, c + 1, j : j + 1] * after(west[c], west[c + 1])
            )
        tail = jnp.where(lane < 124, pltpu.roll(west[3], 124, 1), 0.0)
        late_east[j] = parts[0, 4, j : j + 1] * east[3] + parts[1, 4, j : j + 1] * tail
        front = parts[1, 0, j : j + 1] * pltpu.roll(west[0], 124, 1)
        late_west[j] = before(front, joint[0])
        for c in range(3):
            moved[c, 4 * j + 3] = joint[c].astype(bf16)
            follower = joint[c + 1] if c < 2 else late_east[j]
            moved[c + 1, 4 * j] = before(joint[c], follower).astype(bf16)

    leave = []

    def put(c):
        block = moved[c].reshape(1024, 128).T
        out[32 * c : 32 * c + 32] = block.reshape(32, 4, 1024)
        copy = pltpu.make_async_copy(
            out.at[32 * c : 32 * c + 32], o_hbm.at[32 * c : 32 * c + 32], out_sem.at[c]
        )
        copy.start()
        leave.append(copy)

    put(1)
    put(2)
    last_a.wait()
    last_b.wait()
    outside = jnp.transpose(edges[...].astype(f32))
    for j in range(4):
        mine = outside[64 * j : 64 * j + 64]
        reach = jnp.where(lane < 124, 0.0, pltpu.roll(mine, 124, 1))
        moved[3, 4 * j + 3] = (late_east[j] + parts[1, 4, j : j + 1] * reach).astype(bf16)
        reach = jnp.where(lane < 4, pltpu.roll(parts[0, 0, j : j + 1] * mine, 4, 1), 0.0)
        moved[0, 4 * j] = (late_west[j] + reach).astype(bf16)
    put(0)
    put(3)
    for copy in leave:
        copy.wait()


def solution(mesh):
    peers_elem, peers_lev = mesh.shape["elem"], mesh.shape["lev"]

    def on_device(tracers, velocity, node_mass, source):
        elements = tracers.shape[0]
        anywhere = pl.BlockSpec(memory_space=pl.ANY)
        out = pl.pallas_call(
            functools.partial(kernel, peers_elem, peers_lev, elements * peers_elem),
            out_shape=jax.ShapeDtypeStruct(tracers.shape, bf16),
            in_specs=[anywhere] * 4,
            out_specs=anywhere,
            scratch_shapes=[
                pltpu.VMEM(tracers.shape, bf16),
                pltpu.VMEM(velocity.shape, f32),
                pltpu.VMEM(node_mass.shape, f32),
                pltpu.VMEM((1, elements), jnp.int32),
                pltpu.VMEM(tracers.shape, bf16),
                pltpu.VMEM((16, 64, 512), bf16),
                pltpu.VMEM((4, 48, 128), f32),
                pltpu.VMEM((4, 24, 128), f32),
                pltpu.VMEM((24, 128), f32),
                pltpu.VMEM((24, 128), f32),
                pltpu.VMEM((24, 128), f32),
                pltpu.VMEM((24, 128), f32),
                pltpu.VMEM((CH, 16 * TQ, 128), bf16),
                pltpu.VMEM((CH, 16 * TQ, 128), bf16),
                pltpu.VMEM((CH, 16 * TQ, 512), bf16),
                pltpu.VMEM((CH, 16 * TQ, 128), bf16),
                pltpu.VMEM((CH, 16 * TQ, 128), bf16),
                pltpu.VMEM((CH, 16 * TQ, 128), bf16),
                pltpu.VMEM((CH, 16 * TQ, 128), bf16),
                pltpu.VMEM((CH, 4, 16 * TQ, 128), bf16),
                pltpu.VMEM((4, 256, 128), f32),
                pltpu.VMEM((4, 16, 64, 128), bf16),
                pltpu.VMEM((16, 256), bf16),
                pltpu.VMEM((16, 256), bf16),
                pltpu.VMEM((128, 256), bf16),
                pltpu.VMEM((4, 256, 128), bf16),
                pltpu.VMEM((2, 256, 128), bf16),
                pltpu.VMEM((2, 512, 256), bf16),
                pltpu.VMEM((2, 5, 8, 128), f32),
                pltpu.VMEM((4, 64, 128), f32),
                pltpu.VMEM((4, 64, 128), f32),
                pltpu.SemaphoreType.DMA((4,)),
                pltpu.SemaphoreType.DMA((4,)),
                pltpu.SemaphoreType.DMA((2, 2)),
                pltpu.SemaphoreType.DMA((CH, 2)),
                pltpu.SemaphoreType.DMA((CH, 2, 2)),
                pltpu.SemaphoreType.DMA((2, 2)),
            ],
            compiler_params=pltpu.CompilerParams(collective_id=0, has_side_effects=True),
            name="transport",
        )(
            tracers,
            velocity,
            node_mass,
            source.reshape(1, elements),
        )
        return out

    placed = (P("elem", "lev", None), P(None, None, "lev", "elem"), P(None, "elem"), P("elem"))
    return jax.shard_map(
        on_device, mesh=mesh, in_specs=placed, out_specs=P("elem", "lev", None), check_vma=False
    )
```

```python
import functools

import jax
import jax.numpy as jnp
from jax import lax
from jax.experimental import pallas as pl
from jax.experimental.pallas import tpu as pltpu
from jax.sharding import PartitionSpec as P

MESH = pl.DeviceIdType.MESH
gll = (-1.0, -0.4472135954999579, 0.4472135954999579, 1.0)
courant = 0.15
f32 = jnp.float32
bf16 = jnp.bfloat16
CH = 4
TQ = 64 // CH


def dot(a, b):
    return lax.dot_general(a, b, (((1,), (0,)), ((), ())), preferred_element_type=f32)


def dot_t(a, b):
    return lax.dot_general(a, b, (((1,), (1,)), ((), ())), preferred_element_type=f32)


def three(x):
    top = x.astype(bf16)
    rest = x - top.astype(f32)
    middle = rest.astype(bf16)
    low = (rest - middle.astype(f32)).astype(bf16)
    return [top, middle, low]


def iota(shape, dim):
    return lax.broadcasted_iota(jnp.int32, shape, dim)


def one_hot(rows, code):
    return jnp.where(iota((rows, code.shape[1]), 0) == code, 1.0, 0.0).astype(bf16)


def basis(x):
    out = []
    for a in range(4):
        others = [b for b in range(4) if b != a]
        scale = 1.0
        for b in others:
            scale = scale / (gll[a] - gll[b])
        f = (x - gll[others[0]]) * (x - gll[others[1]]) * (x - gll[others[2]]) * scale
        out.append(f)
    return out


def kernel(
    peers_elem, peers_lev, total,
    t_hbm, v_hbm, mass_hbm, src_hbm, moved, outside, parts,
    t_ref, v_ref, mass_ref, src_ref,
    tt, wind, massx, msg_to_next, msg_to_prev, msg_prev, msg_next,
    x3_send, x3_recv, lifted, pack_next, pack_prev, halo_prev, halo_next,
    gath, wtab, far_send, far_recv, far_pick, far_wtab,
    enter, ask, pick_here,
    in_sem, msg_sem, x3_sem, halo_sem, far_sem,
):
    elem = lax.axis_index("elem")
    lev = lax.axis_index("lev")
    nxt = lax.rem(elem + 1, peers_elem)
    prv = lax.rem(elem + peers_elem - 1, peers_elem)
    below = lax.rem(lev + 1, peers_lev)
    above = lax.rem(lev + peers_lev - 1, peers_lev)

    barrier = pltpu.get_barrier_semaphore()
    for target in ({"elem": nxt}, {"elem": prv}, {"lev": below}, {"lev": above}):
        pl.semaphore_signal(barrier, inc=1, device_id=target, device_id_type=MESH)

    def arrive(i, src, dst):
        copy = pltpu.make_async_copy(src, dst, in_sem.at[i])
        copy.start()
        return copy

    small = [arrive(1, v_hbm, v_ref), arrive(2, mass_hbm, mass_ref), arrive(3, src_hbm, src_ref)]
    large = arrive(0, t_hbm, t_ref)

    def remote(src, dst, sems, target):
        return pltpu.make_async_remote_copy(
            src_ref=src, dst_ref=dst, send_sem=sems.at[0], recv_sem=sems.at[1],
            device_id=target, device_id_type=MESH,
        )

    lane = iota((1, 128), 1)
    level = jnp.bitwise_and(lane, 3)

    def col(c):
        return slice(128 * c, 128 * (c + 1))

    for copy in small:
        copy.wait()
    rel = src_ref[...] - elem * 128 + 64
    rel = jnp.where(rel < 0, rel + total, rel)
    rel = jnp.where(rel >= total, rel - total, rel)
    rel16 = jnp.broadcast_to(rel.astype(f32), (16, 128)).astype(bf16)
    wide_lane = iota((128, 512), 1)
    wide_row = iota((128, 512), 0)
    spread_all = jnp.where(wide_row == jnp.right_shift(wide_lane, 2), 1.0, 0.0).astype(bf16)
    slow = dot(jnp.concatenate(three(mass_ref[...]) + [rel16], axis=0), spread_all)
    mass_wide = slow[0:16] + slow[16:32] + slow[32:48]
    rel_wide = slow[48:56]
    rows = jnp.concatenate(
        [
            jnp.concatenate([v_ref[comp, :, k, :] for comp in range(3)], axis=0)
            for k in range(4)
        ],
        axis=1,
    )
    spread = jnp.concatenate(
        [jnp.where(wide_row * 4 + k == wide_lane, 1.0, 0.0).astype(bf16) for k in range(4)], axis=0
    )
    fast = dot(jnp.concatenate(three(rows), axis=0), spread)
    fast = fast[0:48] + fast[48:96] + fast[96:144]
    for c in range(4):
        wind[c] = fast[:, col(c)]
        massx[c, 0:16, :] = mass_wide[:, col(c)]
        massx[c, 16:24, :] = rel_wide[:, col(c)]

    def side(ref, base, first, c):
        return ref[c, pl.ds(base + first, 4, stride=4), :]

    for message, first, c in ((msg_to_next, 3, 3), (msg_to_prev, 0, 0)):
        message[0:4, :] = side(wind, 0, first, c)
        message[4:8, :] = side(wind, 16, first, c)
        message[8:12, :] = side(massx, 0, first, c)
        message[12:16, :] = side(massx, 0, first, c)
        message[16:24, :] = massx[c, 16:24, :]

    large.wait()
    for block in range(8):
        turned = t_ref[:, :, 128 * block : 128 * (block + 1)].reshape(512, 128).T
        tt[2 * block : 2 * block + 2, :, :] = turned.reshape(2, 64, 512)

    pick = jnp.where(iota((512, 128), 0) == iota((512, 128), 1) * 4 + 3, 1.0, 0.0).astype(bf16)

    def x3_copy(q):
        return remote(x3_send.at[q], x3_recv.at[q], x3_sem.at[q], {"lev": below})

    chosen = dot(tt[...].reshape(1024, 512), pick).astype(bf16).reshape(16, 64, 128)
    for q in range(CH):
        x3_send[q] = chosen[:, TQ * q : TQ * (q + 1), :].reshape(16 * TQ, 128)
        far_recv[q, 16:112, :] = jnp.zeros((96, 16 * TQ), bf16)

    pl.semaphore_wait(barrier, 4)
    send_a = remote(msg_to_next, msg_prev, msg_sem.at[0], {"elem": nxt})
    send_b = remote(msg_to_prev, msg_next, msg_sem.at[1], {"elem": prv})
    send_a.start()
    send_b.start()
    for q in range(CH):
        x3_copy(q).start()

    for c in range(4):
        wind[c, 32:48, :] = 1.0 / (1.0 + jnp.exp(-wind[c, 32:48, :]))

    def code(row, shift):
        return (row.astype(jnp.int32) + shift) * 4 + level

    has_above = jnp.where(lev > 0, 1.0, 0.0)
    step_down = (iota((128, 128), 0) + 1 == iota((128, 128), 1)) & (level != 0)
    for c in range(4):
        enter[c, 0:128, :] = jnp.where(step_down, 1.0, 0.0).astype(bf16)
        entry = iota((128, 128), 0) * 4 - 128 * c == iota((128, 128), 1)
        enter[c, 128:256, :] = (jnp.where(entry, 1.0, 0.0) * has_above).astype(bf16)
    for i, pair in enumerate(((1, 2), (0, 3))):
        for side_of, c in enumerate(pair):
            pick_here[i, :, col(side_of)] = one_hot(512, code(massx[c, 16:17, :], -64))

    eye = jnp.where(iota((128, 128), 0) == iota((128, 128), 1), 1.0, 0.0).astype(bf16)
    far_pick[0:16, :] = dot_t(eye[0:16], pick_here[1, :, 0:128]).astype(bf16)
    far_pick[16:32, :] = dot_t(eye[112:128], pick_here[1, :, 128:256]).astype(bf16)

    def sends(q):
        ahead, back = {"elem": nxt}, {"elem": prv}
        return (
            remote(far_send.at[q, 0], far_recv.at[q, 0:16], far_sem.at[q, 0], back),
            remote(far_send.at[q, 1], far_recv.at[q, 112:128], far_sem.at[q, 1], ahead),
            remote(pack_next.at[q], halo_prev.at[q], halo_sem.at[q, 0], ahead),
            remote(pack_prev.at[q], halo_next.at[q], halo_sem.at[q, 1], back),
        )

    def lift(q):
        rows = pl.ds(pl.multiple_of(q * TQ, TQ), TQ)
        x3_copy(q).wait()
        extra = x3_recv[q]
        for c in range(4):
            here = tt[:, rows, col(c)].reshape(16 * TQ, 128)
            upper = dot(jnp.concatenate([here, extra], axis=1), enter[c])
            descent = jnp.broadcast_to(wind[c, 32:48, :][:, None, :], (16, TQ, 128)).reshape(16 * TQ, 128)
            value = (1.0 - descent) * here.astype(f32) + descent * upper
            lifted[q, :, col(c)] = value.astype(bf16)

    def pack(q):
        pack_next[q] = dot(lifted[q, :, 256:512], ask[0]).astype(bf16)
        pack_prev[q] = dot(lifted[q, :, 0:256], ask[1]).astype(bf16)
        far = dot_t(far_pick[...], lifted[q]).astype(bf16)
        far_send[q, 0] = far[0:16]
        far_send[q, 1] = far[16:32]
        for copy in sends(q):
            copy.start()

    lift(0)
    send_a.wait()
    send_b.wait()
    ask[0] = one_hot(256, code(msg_next[16:17, :], 0))
    ask[1] = one_hot(256, code(msg_prev[16:17, :], -192))

    def step(q, carry):
        pack(q)
        lift(q + 1)
        return carry

    lax.fori_loop(0, CH - 1, step, 0)
    pack(CH - 1)

    def pair(ref, first, c, rows):
        return jnp.concatenate([side(ref, base, first, c) for base in rows], axis=0)

    def after(a, b):
        return jnp.where(lane < 124, pltpu.roll(a, 124, 1), pltpu.roll(b, 124, 1))

    def before(a, b):
        return jnp.where(lane < 4, pltpu.roll(a, 4, 1), pltpu.roll(b, 4, 1))

    wind_east = [msg_prev[0:8, :]] + [pair(wind, 3, c, (0, 16)) for c in range(4)]
    wind_west = [pair(wind, 0, c, (0, 16)) for c in range(4)] + [msg_next[0:8, :]]
    mass_east = [msg_prev[8:16, :]] + [pair(massx, 3, c, (0, 0)) for c in range(4)]
    mass_west = [pair(massx, 0, c, (0, 0)) for c in range(4)] + [msg_next[8:16, :]]
    west_now = [wind_west[0]] + wind_west[:4]
    mass_now = [mass_west[0]] + mass_west[:4]
    shared = []
    for i in range(5):
        mass_next = after(mass_now[i], mass_west[i])
        wind_next = after(west_now[i], wind_west[i])
        inverse = 1.0 / (mass_east[i] + mass_next)
        parts[0, i] = mass_east[i] * inverse
        parts[1, i] = mass_next * inverse
        shared.append((mass_east[i] * wind_east[i] + mass_next * wind_next) * inverse)
    for c in range(4):
        new_west = before(shared[c], shared[c + 1])
        for comp in range(2):
            wind[c, pl.ds(16 * comp + 3, 4, stride=4), :] = shared[c + 1][4 * comp : 4 * comp + 4]
            wind[c, pl.ds(16 * comp, 4, stride=4), :] = new_west[4 * comp : 4 * comp + 4]

    node = iota((16, 1), 0)

    def point(i):
        value = jnp.full(i.shape, gll[3], f32)
        for a in range(3):
            value = jnp.where(i == a, gll[a], value)
        return value

    along_point = point(jnp.bitwise_and(node, 3))
    across_point = point(jnp.right_shift(node, 2))
    for c in range(4):
        along = basis(along_point - courant * wind[c, 0:16, :])
        across = basis(across_point - courant * wind[c, 16:32, :])
        for m in range(16):
            product = across[m // 4] * along[m % 4]
            wtab[c, 16 * m : 16 * m + 16, :] = product.astype(bf16).astype(f32)

    beyond = jnp.where(lane < 4, pltpu.roll(shared[4], 4, 1), shared[0])
    along = basis(jnp.where(lane < 4, gll[0], gll[3]) - courant * beyond[0:4])
    across = basis(point(iota((4, 1), 0)) - courant * beyond[4:8])
    for m in range(16):
        product = across[m // 4] * along[m % 4]
        far_wtab[4 * m : 4 * m + 4, :] = product.astype(bf16).astype(f32)

    def gather(q, carry):
        for i, columns in enumerate(((1, 2), (0, 3))):
            block = dot(lifted[q], pick_here[i]).astype(bf16)
            for half, c in enumerate(columns):
                gath[q, c] = block[:, col(half)]
        return carry

    lax.fori_loop(0, CH, gather, 0)

    def move(q, c, block):
        rows = pl.ds(pl.multiple_of(q * TQ, TQ), TQ)
        values = [block[TQ * m : TQ * (m + 1), :] for m in range(16)]
        for n in range(16):
            total_n = None
            for m in range(16):
                term = wtab[c, pl.ds(16 * m + n, 1), :] * values[m]
                total_n = term if total_n is None else total_n + term
            moved[c, n, rows, :] = total_n.astype(bf16)

    def inner(i, carry):
        q, c = i // 2, lax.rem(i, 2) + 1
        move(q, c, gath[q, c].astype(f32))
        return carry

    lax.fori_loop(0, 2 * CH, inner, 0)

    def outer(q, carry):
        rows = pl.ds(pl.multiple_of(q * TQ, TQ), TQ)
        for copy in sends(q):
            copy.wait()
        move(q, 0, gath[q, 0].astype(f32) + halo_prev[q].astype(f32))
        move(q, 3, gath[q, 3].astype(f32) + halo_next[q].astype(f32))
        here = jnp.where(lane < 64, pack_next[q].astype(f32), pack_prev[q].astype(f32))
        block = jnp.transpose(far_recv[q].astype(f32))
        block = jnp.where((lane < 4) | (lane >= 124), block + here, 0.0)
        values = [block[TQ * m : TQ * (m + 1), :] for m in range(16)]
        for j in range(4):
            total_j = None
            for m in range(16):
                term = far_wtab[pl.ds(4 * m + j, 1), :] * values[m]
                total_j = term if total_j is None else total_j + term
            outside[j, rows, :] = total_j.astype(bf16)
        return carry

    lax.fori_loop(0, CH, outer, 0)


def share_kernel(moved, outside, parts, o_hbm, out, out_sem):
    lane = iota((1, 128), 1)

    def after(a, b):
        return jnp.where(lane < 124, pltpu.roll(a, 124, 1), pltpu.roll(b, 124, 1))

    def before(a, b):
        return jnp.where(lane < 4, pltpu.roll(a, 4, 1), pltpu.roll(b, 4, 1))

    leave = []
    for j in range(4):
        mine = outside[j].astype(f32)
        east = [mine] + [moved[c, 4 * j + 3].astype(f32) for c in range(4)]
        west = [moved[c, 4 * j].astype(f32) for c in range(4)] + [mine]
        now = [west[0]] + west[:4]
        joint = [
            parts[0, i, j : j + 1] * east[i] + parts[1, i, j : j + 1] * after(now[i], west[i])
            for i in range(5)
        ]
        for c in range(4):
            first = before(joint[c], joint[c + 1]).astype(bf16)
            last = joint[c + 1].astype(bf16)
            for half, pair in enumerate(((first, moved[c, 4 * j + 1]), (moved[c, 4 * j + 2], last))):
                turned = jnp.concatenate(pair, axis=0).T
                place = slice(256 * j + 128 * half, 256 * j + 128 * half + 128)
                out[32 * c : 32 * c + 32, :, place] = turned.reshape(32, 4, 128)
        place = slice(256 * j, 256 * j + 256)
        copy = pltpu.make_async_copy(out.at[:, :, place], o_hbm.at[:, :, place], out_sem.at[j])
        copy.start()
        leave.append(copy)
    for copy in leave:
        copy.wait()


def solution(mesh):
    peers_elem, peers_lev = mesh.shape["elem"], mesh.shape["lev"]

    def on_device(tracers, velocity, node_mass, source):
        elements = tracers.shape[0]
        anywhere = pl.BlockSpec(memory_space=pl.ANY)
        vmem = pl.BlockSpec(memory_space=pltpu.VMEM)
        pieces = pl.pallas_call(
            functools.partial(kernel, peers_elem, peers_lev, elements * peers_elem),
            out_shape=(
                pltpu.VMEM((4, 16, 64, 128), bf16),
                pltpu.VMEM((4, 64, 128), bf16),
                pltpu.VMEM((2, 5, 8, 128), f32),
            ),
            in_specs=[anywhere] * 4,
            out_specs=(vmem, vmem, vmem),
            scratch_shapes=[
                pltpu.VMEM(tracers.shape, bf16),
                pltpu.VMEM(velocity.shape, f32),
                pltpu.VMEM(node_mass.shape, f32),
                pltpu.VMEM((1, elements), jnp.int32),
                pltpu.VMEM((16, 64, 512), bf16),
                pltpu.VMEM((4, 48, 128), f32),
                pltpu.VMEM((4, 24, 128), f32),
                pltpu.VMEM((24, 128), f32),
                pltpu.VMEM((24, 128), f32),
                pltpu.VMEM((24, 128), f32),
                pltpu.VMEM((24, 128), f32),
                pltpu.VMEM((CH, 16 * TQ, 128), bf16),
                pltpu.VMEM((CH, 16 * TQ, 128), bf16),
                pltpu.VMEM((CH, 16 * TQ, 512), bf16),
                pltpu.VMEM((CH, 16 * TQ, 128), bf16),
                pltpu.VMEM((CH, 16 * TQ, 128), bf16),
                pltpu.VMEM((CH, 16 * TQ, 128), bf16),
                pltpu.VMEM((CH, 16 * TQ, 128), bf16),
                pltpu.VMEM((CH, 4, 16 * TQ, 128), bf16),
                pltpu.VMEM((4, 256, 128), f32),
                pltpu.VMEM((CH, 2, 16, 16 * TQ), bf16),
                pltpu.VMEM((CH, 128, 16 * TQ), bf16),
                pltpu.VMEM((32, 512), bf16),
                pltpu.VMEM((64, 128), f32),
                pltpu.VMEM((4, 256, 128), bf16),
                pltpu.VMEM((2, 256, 128), bf16),
                pltpu.VMEM((2, 512, 256), bf16),
                pltpu.SemaphoreType.DMA((4,)),
                pltpu.SemaphoreType.DMA((2, 2)),
                pltpu.SemaphoreType.DMA((CH, 2)),
                pltpu.SemaphoreType.DMA((CH, 2, 2)),
                pltpu.SemaphoreType.DMA((CH, 2, 2)),
            ],
            compiler_params=pltpu.CompilerParams(collective_id=0, has_side_effects=True),
            name="transport",
        )(tracers, velocity, node_mass, source.reshape(1, elements))
        return pl.pallas_call(
            share_kernel,
            out_shape=jax.ShapeDtypeStruct(tracers.shape, bf16),
            in_specs=[vmem] * 3,
            out_specs=anywhere,
            scratch_shapes=[pltpu.VMEM(tracers.shape, bf16), pltpu.SemaphoreType.DMA((4,))],
            compiler_params=pltpu.CompilerParams(vmem_limit_bytes=24 * 2**20),
            name="share",
        )(*pieces)

    placed = (P("elem", "lev", None), P(None, None, "lev", "elem"), P(None, "elem"), P("elem"))
    return jax.shard_map(
        on_device, mesh=mesh, in_specs=placed, out_specs=P("elem", "lev", None), check_vma=False
    )
```

```python
import functools

import jax
import jax.numpy as jnp
from jax import lax
from jax.experimental import pallas as pl
from jax.experimental.pallas import tpu as pltpu
from jax.sharding import PartitionSpec as P

MESH = pl.DeviceIdType.MESH
gll = (-1.0, -0.4472135954999579, 0.4472135954999579, 1.0)
courant = 0.15
f32 = jnp.float32
bf16 = jnp.bfloat16
CH = 4
TQ = 64 // CH


def dot(a, b):
    return lax.dot_general(a, b, (((1,), (0,)), ((), ())), preferred_element_type=f32)


def dot_t(a, b):
    return lax.dot_general(a, b, (((1,), (1,)), ((), ())), preferred_element_type=f32)


def three(x):
    top = x.astype(bf16)
    rest = x - top.astype(f32)
    middle = rest.astype(bf16)
    low = (rest - middle.astype(f32)).astype(bf16)
    return [top, middle, low]


def iota(shape, dim):
    return lax.broadcasted_iota(jnp.int32, shape, dim)


def one_hot(rows, code):
    return jnp.where(iota((rows, code.shape[1]), 0) == code, 1.0, 0.0).astype(bf16)


def basis(x):
    out = []
    for a in range(4):
        others = [b for b in range(4) if b != a]
        scale = 1.0
        for b in others:
            scale = scale / (gll[a] - gll[b])
        f = (x - gll[others[0]]) * (x - gll[others[1]]) * (x - gll[others[2]]) * scale
        out.append(f)
    return out


def kernel(
    peers_elem, peers_lev, total,
    t_hbm, v_hbm, mass_hbm, src_hbm, moved, outside, parts,
    t_ref, v_ref, mass_ref, src_ref,
    tt, wind, massx, msg_to_next, msg_to_prev, msg_prev, msg_next,
    x3_send, x3_recv, lifted, pack_next, pack_prev, halo_prev, halo_next,
    gath, wtab, far_send, far_recv, far_pick, far_wtab,
    enter, ask, pick_here, full_prev, full_next,
    in_sem, msg_sem, x3_sem, halo_sem, far_sem, full_sem,
):
    elem = lax.axis_index("elem")
    lev = lax.axis_index("lev")
    nxt = lax.rem(elem + 1, peers_elem)
    prv = lax.rem(elem + peers_elem - 1, peers_elem)
    below = lax.rem(lev + 1, peers_lev)
    above = lax.rem(lev + peers_lev - 1, peers_lev)

    barrier = pltpu.get_barrier_semaphore()
    for target in ({"elem": nxt}, {"elem": prv}, {"lev": below}, {"lev": above}):
        pl.semaphore_signal(barrier, inc=1, device_id=target, device_id_type=MESH)

    def arrive(i, src, dst):
        copy = pltpu.make_async_copy(src, dst, in_sem.at[i])
        copy.start()
        return copy

    small = [arrive(1, v_hbm, v_ref), arrive(2, mass_hbm, mass_ref), arrive(3, src_hbm, src_ref)]
    large = arrive(0, t_hbm, t_ref)

    def remote(src, dst, sems, target):
        return pltpu.make_async_remote_copy(
            src_ref=src, dst_ref=dst, send_sem=sems.at[0], recv_sem=sems.at[1],
            device_id=target, device_id_type=MESH,
        )

    lane = iota((1, 128), 1)
    level = jnp.bitwise_and(lane, 3)

    def col(c):
        return slice(128 * c, 128 * (c + 1))

    for copy in small:
        copy.wait()
    rel = src_ref[...] - elem * 128 + 64
    rel = jnp.where(rel < 0, rel + total, rel)
    rel = jnp.where(rel >= total, rel - total, rel)
    rel16 = jnp.broadcast_to(rel.astype(f32), (16, 128)).astype(bf16)
    wide_lane = iota((128, 512), 1)
    wide_row = iota((128, 512), 0)
    spread_all = jnp.where(wide_row == jnp.right_shift(wide_lane, 2), 1.0, 0.0).astype(bf16)
    slow = dot(jnp.concatenate(three(mass_ref[...]) + [rel16], axis=0), spread_all)
    mass_wide = slow[0:16] + slow[16:32] + slow[32:48]
    rel_wide = slow[48:56]
    rows = jnp.concatenate(
        [
            jnp.concatenate([v_ref[comp, :, k, :] for comp in range(3)], axis=0)
            for k in range(4)
        ],
        axis=1,
    )
    spread = jnp.concatenate(
        [jnp.where(wide_row * 4 + k == wide_lane, 1.0, 0.0).astype(bf16) for k in range(4)], axis=0
    )
    fast = dot(jnp.concatenate(three(rows), axis=0), spread)
    fast = fast[0:48] + fast[48:96] + fast[96:144]
    for c in range(4):
        wind[c] = fast[:, col(c)]
        massx[c, 0:16, :] = mass_wide[:, col(c)]
        massx[c, 16:24, :] = rel_wide[:, col(c)]

    def side(ref, base, first, c):
        return ref[c, pl.ds(base + first, 4, stride=4), :]

    for message, first, c in ((msg_to_next, 3, 3), (msg_to_prev, 0, 0)):
        message[0:4, :] = side(wind, 0, first, c)
        message[4:8, :] = side(wind, 16, first, c)
        message[8:12, :] = side(massx, 0, first, c)
        message[12:16, :] = side(massx, 0, first, c)
        message[16:24, :] = massx[c, 16:24, :]

    large.wait()
    for block in range(8):
        turned = t_ref[:, :, 128 * block : 128 * (block + 1)].reshape(512, 128).T
        tt[2 * block : 2 * block + 2, :, :] = turned.reshape(2, 64, 512)

    pick = jnp.where(iota((512, 128), 0) == iota((512, 128), 1) * 4 + 3, 1.0, 0.0).astype(bf16)

    def x3_copy(q):
        return remote(x3_send.at[q], x3_recv.at[q], x3_sem.at[q], {"lev": below})

    chosen = dot(tt[...].reshape(1024, 512), pick).astype(bf16).reshape(16, 64, 128)
    for q in range(CH):
        x3_send[q] = chosen[:, TQ * q : TQ * (q + 1), :].reshape(16 * TQ, 128)
        far_recv[q, 16:112, :] = jnp.zeros((96, 16 * TQ), bf16)

    pl.semaphore_wait(barrier, 4)
    send_a = remote(msg_to_next, msg_prev, msg_sem.at[0], {"elem": nxt})
    send_b = remote(msg_to_prev, msg_next, msg_sem.at[1], {"elem": prv})
    send_a.start()
    send_b.start()
    for q in range(CH):
        x3_copy(q).start()

    for c in range(4):
        wind[c, 32:48, :] = 1.0 / (1.0 + jnp.exp(-wind[c, 32:48, :]))

    def code(row, shift):
        return (row.astype(jnp.int32) + shift) * 4 + level

    has_above = jnp.where(lev > 0, 1.0, 0.0)
    step_down = (iota((128, 128), 0) + 1 == iota((128, 128), 1)) & (level != 0)
    for c in range(4):
        enter[c, 0:128, :] = jnp.where(step_down, 1.0, 0.0).astype(bf16)
        entry = iota((128, 128), 0) * 4 - 128 * c == iota((128, 128), 1)
        enter[c, 128:256, :] = (jnp.where(entry, 1.0, 0.0) * has_above).astype(bf16)
    for i, pair in enumerate(((1, 2), (0, 3))):
        for side_of, c in enumerate(pair):
            pick_here[i, :, col(side_of)] = one_hot(512, code(massx[c, 16:17, :], -64))

    eye = jnp.where(iota((128, 128), 0) == iota((128, 128), 1), 1.0, 0.0).astype(bf16)
    far_pick[0:16, :] = dot_t(eye[0:16], pick_here[1, :, 0:128]).astype(bf16)
    far_pick[16:32, :] = dot_t(eye[112:128], pick_here[1, :, 128:256]).astype(bf16)

    ahead, back = {"elem": nxt}, {"elem": prv}

    def from_next(q):
        return remote(pack_prev.at[q], halo_next.at[q], halo_sem.at[q, 1], back)

    def from_prev(q):
        return remote(pack_next.at[q], halo_prev.at[q], halo_sem.at[q, 0], ahead)

    def far_copies(q):
        return (
            remote(far_send.at[q, 0], far_recv.at[q, 0:16], far_sem.at[q, 0], back),
            remote(far_send.at[q, 1], far_recv.at[q, 112:128], far_sem.at[q, 1], ahead),
        )

    full_ahead = remote(lifted.at[0, :, 256:512], full_prev, full_sem.at[0], ahead)
    full_back = remote(lifted.at[0, :, 0:256], full_next, full_sem.at[1], back)

    def lift(q):
        rows = pl.ds(pl.multiple_of(q * TQ, TQ), TQ)
        x3_copy(q).wait()
        extra = x3_recv[q]
        for c in range(4):
            here = tt[:, rows, col(c)].reshape(16 * TQ, 128)
            upper = dot(jnp.concatenate([here, extra], axis=1), enter[c])
            descent = jnp.broadcast_to(wind[c, 32:48, :][:, None, :], (16, TQ, 128)).reshape(16 * TQ, 128)
            value = (1.0 - descent) * here.astype(f32) + descent * upper
            lifted[q, :, col(c)] = value.astype(bf16)

    def far_out(q):
        far = dot_t(far_pick[...], lifted[q]).astype(bf16)
        far_send[q, 0] = far[0:16]
        far_send[q, 1] = far[16:32]
        for copy in far_copies(q):
            copy.start()

    def pack(q):
        pack_next[q] = dot(lifted[q, :, 256:512], ask[0]).astype(bf16)
        pack_prev[q] = dot(lifted[q, :, 0:256], ask[1]).astype(bf16)

    lift(0)
    full_ahead.start()
    full_back.start()
    far_out(0)

    def lift_more(q, carry):
        lift(q)
        far_out(q)
        return carry

    lax.fori_loop(1, CH, lift_more, 0)
    send_a.wait()
    send_b.wait()
    ask[0] = one_hot(256, code(msg_next[16:17, :], 0))
    ask[1] = one_hot(256, code(msg_prev[16:17, :], -192))

    def answer(q, carry):
        pack(q)
        from_prev(q).start()
        from_next(q).start()
        return carry

    lax.fori_loop(1, CH, answer, 0)
    pack(0)
    ask[2] = one_hot(256, code(massx[0, 16:17, :], 0))
    ask[3] = one_hot(256, code(massx[3, 16:17, :], -192))

    def pair(ref, first, c, rows):
        return jnp.concatenate([side(ref, base, first, c) for base in rows], axis=0)

    def after(a, b):
        return jnp.where(lane < 124, pltpu.roll(a, 124, 1), pltpu.roll(b, 124, 1))

    def before(a, b):
        return jnp.where(lane < 4, pltpu.roll(a, 4, 1), pltpu.roll(b, 4, 1))

    wind_east = [msg_prev[0:8, :]] + [pair(wind, 3, c, (0, 16)) for c in range(4)]
    wind_west = [pair(wind, 0, c, (0, 16)) for c in range(4)] + [msg_next[0:8, :]]
    mass_east = [msg_prev[8:16, :]] + [pair(massx, 3, c, (0, 0)) for c in range(4)]
    mass_west = [pair(massx, 0, c, (0, 0)) for c in range(4)] + [msg_next[8:16, :]]
    west_now = [wind_west[0]] + wind_west[:4]
    mass_now = [mass_west[0]] + mass_west[:4]
    shared = []
    for i in range(5):
        mass_next = after(mass_now[i], mass_west[i])
        wind_next = after(west_now[i], wind_west[i])
        inverse = 1.0 / (mass_east[i] + mass_next)
        parts[0, i] = mass_east[i] * inverse
        parts[1, i] = mass_next * inverse
        shared.append((mass_east[i] * wind_east[i] + mass_next * wind_next) * inverse)
    for c in range(4):
        new_west = before(shared[c], shared[c + 1])
        for comp in range(2):
            wind[c, pl.ds(16 * comp + 3, 4, stride=4), :] = shared[c + 1][4 * comp : 4 * comp + 4]
            wind[c, pl.ds(16 * comp, 4, stride=4), :] = new_west[4 * comp : 4 * comp + 4]

    node = iota((16, 1), 0)

    def point(i):
        value = jnp.full(i.shape, gll[3], f32)
        for a in range(3):
            value = jnp.where(i == a, gll[a], value)
        return value

    along_point = point(jnp.bitwise_and(node, 3))
    across_point = point(jnp.right_shift(node, 2))
    for c in range(4):
        along = basis(along_point - courant * wind[c, 0:16, :])
        across = basis(across_point - courant * wind[c, 16:32, :])
        for m in range(16):
            product = across[m // 4] * along[m % 4]
            wtab[c, 16 * m : 16 * m + 16, :] = product.astype(bf16).astype(f32)

    beyond = jnp.where(lane < 4, pltpu.roll(shared[4], 4, 1), shared[0])
    along = basis(jnp.where(lane < 4, gll[0], gll[3]) - courant * beyond[0:4])
    across = basis(point(iota((4, 1), 0)) - courant * beyond[4:8])
    for m in range(16):
        product = across[m // 4] * along[m % 4]
        far_wtab[4 * m : 4 * m + 4, :] = product.astype(bf16).astype(f32)

    def gather(q, carry):
        for i, columns in enumerate(((1, 2), (0, 3))):
            block = dot(lifted[q], pick_here[i]).astype(bf16)
            for half, c in enumerate(columns):
                gath[q, c] = block[:, col(half)]
        return carry

    lax.fori_loop(0, CH, gather, 0)

    def move(q, c, block):
        rows = pl.ds(pl.multiple_of(q * TQ, TQ), TQ)
        values = [block[TQ * m : TQ * (m + 1), :] for m in range(16)]
        for n in range(16):
            total_n = None
            for m in range(16):
                term = wtab[c, pl.ds(16 * m + n, 1), :] * values[m]
                total_n = term if total_n is None else total_n + term
            moved[c, n, rows, :] = total_n.astype(bf16)

    def inner(i, carry):
        q, c = i // 2, lax.rem(i, 2) + 1
        move(q, c, gath[q, c].astype(f32))
        return carry

    lax.fori_loop(0, 2 * CH, inner, 0)

    full_back.wait()
    halo_next[0] = dot(full_next[...], ask[3]).astype(bf16)

    def outer_east(q, carry):
        @pl.when(q > 0)
        def _():
            from_next(q).wait()

        move(q, 3, gath[q, 3].astype(f32) + halo_next[q].astype(f32))
        return carry

    lax.fori_loop(0, CH, outer_east, 0)
    full_ahead.wait()
    halo_prev[0] = dot(full_prev[...], ask[2]).astype(bf16)

    def outer_west(q, carry):
        rows = pl.ds(pl.multiple_of(q * TQ, TQ), TQ)
        for copy in far_copies(q):
            copy.wait()

        @pl.when(q > 0)
        def _():
            from_prev(q).wait()

        move(q, 0, gath[q, 0].astype(f32) + halo_prev[q].astype(f32))
        here = jnp.where(lane < 64, pack_next[q].astype(f32), pack_prev[q].astype(f32))
        block = jnp.transpose(far_recv[q].astype(f32))
        block = jnp.where((lane < 4) | (lane >= 124), block + here, 0.0)
        values = [block[TQ * m : TQ * (m + 1), :] for m in range(16)]
        for j in range(4):
            total_j = None
            for m in range(16):
                term = far_wtab[pl.ds(4 * m + j, 1), :] * values[m]
                total_j = term if total_j is None else total_j + term
            outside[j, rows, :] = total_j.astype(bf16)
        return carry

    lax.fori_loop(0, CH, outer_west, 0)


def share_kernel(moved, outside, parts, o_hbm, out, out_sem):
    lane = iota((1, 128), 1)

    def after(a, b):
        return jnp.where(lane < 124, pltpu.roll(a, 124, 1), pltpu.roll(b, 124, 1))

    def before(a, b):
        return jnp.where(lane < 4, pltpu.roll(a, 4, 1), pltpu.roll(b, 4, 1))

    leave = []
    for j in range(4):
        mine = outside[j].astype(f32)
        east = [mine] + [moved[c, 4 * j + 3].astype(f32) for c in range(4)]
        west = [moved[c, 4 * j].astype(f32) for c in range(4)] + [mine]
        now = [west[0]] + west[:4]
        joint = [
            parts[0, i, j : j + 1] * east[i] + parts[1, i, j : j + 1] * after(now[i], west[i])
            for i in range(5)
        ]
        for c in range(4):
            first = before(joint[c], joint[c + 1]).astype(bf16)
            last = joint[c + 1].astype(bf16)
            for half, pair in enumerate(((first, moved[c, 4 * j + 1]), (moved[c, 4 * j + 2], last))):
                turned = jnp.concatenate(pair, axis=0).T
                place = slice(256 * j + 128 * half, 256 * j + 128 * half + 128)
                out[32 * c : 32 * c + 32, :, place] = turned.reshape(32, 4, 128)
        place = slice(256 * j, 256 * j + 256)
        copy = pltpu.make_async_copy(out.at[:, :, place], o_hbm.at[:, :, place], out_sem.at[j])
        copy.start()
        leave.append(copy)
    for copy in leave:
        copy.wait()


def solution(mesh):
    peers_elem, peers_lev = mesh.shape["elem"], mesh.shape["lev"]

    def on_device(tracers, velocity, node_mass, source):
        elements = tracers.shape[0]
        anywhere = pl.BlockSpec(memory_space=pl.ANY)
        vmem = pl.BlockSpec(memory_space=pltpu.VMEM)
        pieces = pl.pallas_call(
            functools.partial(kernel, peers_elem, peers_lev, elements * peers_elem),
            out_shape=(
                pltpu.VMEM((4, 16, 64, 128), bf16),
                pltpu.VMEM((4, 64, 128), bf16),
                pltpu.VMEM((2, 5, 8, 128), f32),
            ),
            in_specs=[anywhere] * 4,
            out_specs=(vmem, vmem, vmem),
            scratch_shapes=[
                pltpu.VMEM(tracers.shape, bf16),
                pltpu.VMEM(velocity.shape, f32),
                pltpu.VMEM(node_mass.shape, f32),
                pltpu.VMEM((1, elements), jnp.int32),
                pltpu.VMEM((16, 64, 512), bf16),
                pltpu.VMEM((4, 48, 128), f32),
                pltpu.VMEM((4, 24, 128), f32),
                pltpu.VMEM((24, 128), f32),
                pltpu.VMEM((24, 128), f32),
                pltpu.VMEM((24, 128), f32),
                pltpu.VMEM((24, 128), f32),
                pltpu.VMEM((CH, 16 * TQ, 128), bf16),
                pltpu.VMEM((CH, 16 * TQ, 128), bf16),
                pltpu.VMEM((CH, 16 * TQ, 512), bf16),
                pltpu.VMEM((CH, 16 * TQ, 128), bf16),
                pltpu.VMEM((CH, 16 * TQ, 128), bf16),
                pltpu.VMEM((CH, 16 * TQ, 128), bf16),
                pltpu.VMEM((CH, 16 * TQ, 128), bf16),
                pltpu.VMEM((CH, 4, 16 * TQ, 128), bf16),
                pltpu.VMEM((4, 256, 128), f32),
                pltpu.VMEM((CH, 2, 16, 16 * TQ), bf16),
                pltpu.VMEM((CH, 128, 16 * TQ), bf16),
                pltpu.VMEM((32, 512), bf16),
                pltpu.VMEM((64, 128), f32),
                pltpu.VMEM((4, 256, 128), bf16),
                pltpu.VMEM((4, 256, 128), bf16),
                pltpu.VMEM((2, 512, 256), bf16),
                pltpu.VMEM((16 * TQ, 256), bf16),
                pltpu.VMEM((16 * TQ, 256), bf16),
                pltpu.SemaphoreType.DMA((4,)),
                pltpu.SemaphoreType.DMA((2, 2)),
                pltpu.SemaphoreType.DMA((CH, 2)),
                pltpu.SemaphoreType.DMA((CH, 2, 2)),
                pltpu.SemaphoreType.DMA((CH, 2, 2)),
                pltpu.SemaphoreType.DMA((2, 2)),
            ],
            compiler_params=pltpu.CompilerParams(collective_id=0, has_side_effects=True),
            name="transport",
        )(tracers, velocity, node_mass, source.reshape(1, elements))
        return pl.pallas_call(
            share_kernel,
            out_shape=jax.ShapeDtypeStruct(tracers.shape, bf16),
            in_specs=[vmem] * 3,
            out_specs=anywhere,
            scratch_shapes=[pltpu.VMEM(tracers.shape, bf16), pltpu.SemaphoreType.DMA((4,))],
            compiler_params=pltpu.CompilerParams(vmem_limit_bytes=24 * 2**20),
            name="share",
        )(*pieces)

    placed = (P("elem", "lev", None), P(None, None, "lev", "elem"), P(None, "elem"), P("elem"))
    return jax.shard_map(
        on_device, mesh=mesh, in_specs=placed, out_specs=P("elem", "lev", None), check_vma=False
    )
```

```python
import functools

import jax
import jax.numpy as jnp
from jax import lax
from jax.experimental import pallas as pl
from jax.experimental.pallas import tpu as pltpu
from jax.sharding import PartitionSpec as P

MESH = pl.DeviceIdType.MESH
gll = (-1.0, -0.4472135954999579, 0.4472135954999579, 1.0)
courant = 0.15
f32 = jnp.float32
bf16 = jnp.bfloat16
CH = 4
TQ = 64 // CH


def dot(a, b):
    return lax.dot_general(a, b, (((1,), (0,)), ((), ())), preferred_element_type=f32)


def dot_t(a, b):
    return lax.dot_general(a, b, (((1,), (1,)), ((), ())), preferred_element_type=f32)


def three(x):
    top = x.astype(bf16)
    rest = x - top.astype(f32)
    middle = rest.astype(bf16)
    low = (rest - middle.astype(f32)).astype(bf16)
    return [top, middle, low]


def iota(shape, dim):
    return lax.broadcasted_iota(jnp.int32, shape, dim)


def one_hot(rows, code):
    return jnp.where(iota((rows, code.shape[1]), 0) == code, 1.0, 0.0).astype(bf16)


def basis(x):
    out = []
    for a in range(4):
        others = [b for b in range(4) if b != a]
        scale = 1.0
        for b in others:
            scale = scale / (gll[a] - gll[b])
        f = (x - gll[others[0]]) * (x - gll[others[1]]) * (x - gll[others[2]]) * scale
        out.append(f)
    return out


def kernel(
    peers_elem, peers_lev, total,
    t_hbm, v_hbm, mass_hbm, src_hbm, first_col, west_raw, outside, parts, rest,
    t_ref, v_ref, mass_ref, src_ref,
    tt, wind, massx, msg_to_next, msg_to_prev, msg_prev, msg_next,
    x3_send, x3_recv, lifted, pack_next, pack_prev, halo_prev, halo_next,
    gath, wtab, far_send, far_recv, far_pick, far_wtab,
    enter, ask, pick_here, full_prev, full_next, moved,
    in_sem, msg_sem, x3_sem, halo_sem, far_sem, full_sem,
):
    elem = lax.axis_index("elem")
    lev = lax.axis_index("lev")
    nxt = lax.rem(elem + 1, peers_elem)
    prv = lax.rem(elem + peers_elem - 1, peers_elem)
    below = lax.rem(lev + 1, peers_lev)
    above = lax.rem(lev + peers_lev - 1, peers_lev)

    barrier = pltpu.get_barrier_semaphore()
    for target in ({"elem": nxt}, {"elem": prv}, {"lev": below}, {"lev": above}):
        pl.semaphore_signal(barrier, inc=1, device_id=target, device_id_type=MESH)

    def arrive(i, src, dst):
        copy = pltpu.make_async_copy(src, dst, in_sem.at[i])
        copy.start()
        return copy

    small = [arrive(1, v_hbm, v_ref), arrive(2, mass_hbm, mass_ref), arrive(3, src_hbm, src_ref)]
    large = arrive(0, t_hbm, t_ref)

    def remote(src, dst, sems, target):
        return pltpu.make_async_remote_copy(
            src_ref=src, dst_ref=dst, send_sem=sems.at[0], recv_sem=sems.at[1],
            device_id=target, device_id_type=MESH,
        )

    lane = iota((1, 128), 1)
    level = jnp.bitwise_and(lane, 3)

    def col(c):
        return slice(128 * c, 128 * (c + 1))

    for copy in small:
        copy.wait()
    rel = src_ref[...] - elem * 128 + 64
    rel = jnp.where(rel < 0, rel + total, rel)
    rel = jnp.where(rel >= total, rel - total, rel)
    rel16 = jnp.broadcast_to(rel.astype(f32), (16, 128)).astype(bf16)
    wide_lane = iota((128, 512), 1)
    wide_row = iota((128, 512), 0)
    spread_all = jnp.where(wide_row == jnp.right_shift(wide_lane, 2), 1.0, 0.0).astype(bf16)
    slow = dot(jnp.concatenate(three(mass_ref[...]) + [rel16], axis=0), spread_all)
    mass_wide = slow[0:16] + slow[16:32] + slow[32:48]
    rel_wide = slow[48:56]
    rows = jnp.concatenate(
        [
            jnp.concatenate([v_ref[comp, :, k, :] for comp in range(3)], axis=0)
            for k in range(4)
        ],
        axis=1,
    )
    spread = jnp.concatenate(
        [jnp.where(wide_row * 4 + k == wide_lane, 1.0, 0.0).astype(bf16) for k in range(4)], axis=0
    )
    fast = dot(jnp.concatenate(three(rows), axis=0), spread)
    fast = fast[0:48] + fast[48:96] + fast[96:144]
    for c in range(4):
        wind[c] = fast[:, col(c)]
        massx[c, 0:16, :] = mass_wide[:, col(c)]
        massx[c, 16:24, :] = rel_wide[:, col(c)]

    def side(ref, base, first, c):
        return ref[c, pl.ds(base + first, 4, stride=4), :]

    for message, first, c in ((msg_to_next, 3, 3), (msg_to_prev, 0, 0)):
        message[0:4, :] = side(wind, 0, first, c)
        message[4:8, :] = side(wind, 16, first, c)
        message[8:12, :] = side(massx, 0, first, c)
        message[12:16, :] = side(massx, 0, first, c)
        message[16:24, :] = massx[c, 16:24, :]

    large.wait()
    for block in range(8):
        turned = t_ref[:, :, 128 * block : 128 * (block + 1)].reshape(512, 128).T
        tt[2 * block : 2 * block + 2, :, :] = turned.reshape(2, 64, 512)

    pick = jnp.where(iota((512, 128), 0) == iota((512, 128), 1) * 4 + 3, 1.0, 0.0).astype(bf16)

    def x3_copy(q):
        return remote(x3_send.at[q], x3_recv.at[q], x3_sem.at[q], {"lev": below})

    chosen = dot(tt[...].reshape(1024, 512), pick).astype(bf16).reshape(16, 64, 128)
    for q in range(CH):
        x3_send[q] = chosen[:, TQ * q : TQ * (q + 1), :].reshape(16 * TQ, 128)
        far_recv[q, 16:112, :] = jnp.zeros((96, 16 * TQ), bf16)

    pl.semaphore_wait(barrier, 4)
    send_a = remote(msg_to_next, msg_prev, msg_sem.at[0], {"elem": nxt})
    send_b = remote(msg_to_prev, msg_next, msg_sem.at[1], {"elem": prv})
    send_a.start()
    send_b.start()
    for q in range(CH):
        x3_copy(q).start()

    for c in range(4):
        wind[c, 32:48, :] = 1.0 / (1.0 + jnp.exp(-wind[c, 32:48, :]))

    def code(row, shift):
        return (row.astype(jnp.int32) + shift) * 4 + level

    has_above = jnp.where(lev > 0, 1.0, 0.0)
    step_down = (iota((128, 128), 0) + 1 == iota((128, 128), 1)) & (level != 0)
    for c in range(4):
        enter[c, 0:128, :] = jnp.where(step_down, 1.0, 0.0).astype(bf16)
        entry = iota((128, 128), 0) * 4 - 128 * c == iota((128, 128), 1)
        enter[c, 128:256, :] = (jnp.where(entry, 1.0, 0.0) * has_above).astype(bf16)
    for i, pair in enumerate(((1, 2), (0, 3))):
        for side_of, c in enumerate(pair):
            pick_here[i, :, col(side_of)] = one_hot(512, code(massx[c, 16:17, :], -64))

    eye = jnp.where(iota((128, 128), 0) == iota((128, 128), 1), 1.0, 0.0).astype(bf16)
    far_pick[0:16, :] = dot_t(eye[0:16], pick_here[1, :, 0:128]).astype(bf16)
    far_pick[16:32, :] = dot_t(eye[112:128], pick_here[1, :, 128:256]).astype(bf16)

    ahead, back = {"elem": nxt}, {"elem": prv}

    def from_next(q):
        return remote(pack_prev.at[q], halo_next.at[q], halo_sem.at[q, 1], back)

    def from_prev(q):
        return remote(pack_next.at[q], halo_prev.at[q], halo_sem.at[q, 0], ahead)

    def far_copies(q):
        return (
            remote(far_send.at[q, 0], far_recv.at[q, 0:16], far_sem.at[q, 0], back),
            remote(far_send.at[q, 1], far_recv.at[q, 112:128], far_sem.at[q, 1], ahead),
        )

    full_ahead = remote(lifted.at[0, :, 256:512], full_prev, full_sem.at[0], ahead)
    full_back = remote(lifted.at[0, :, 0:256], full_next, full_sem.at[1], back)

    def lift(q):
        rows = pl.ds(pl.multiple_of(q * TQ, TQ), TQ)
        x3_copy(q).wait()
        extra = x3_recv[q]
        for c in range(4):
            here = tt[:, rows, col(c)].reshape(16 * TQ, 128)
            upper = dot(jnp.concatenate([here, extra], axis=1), enter[c])
            descent = jnp.broadcast_to(wind[c, 32:48, :][:, None, :], (16, TQ, 128)).reshape(16 * TQ, 128)
            value = (1.0 - descent) * here.astype(f32) + descent * upper
            lifted[q, :, col(c)] = value.astype(bf16)

    def far_out(q):
        far = dot_t(far_pick[...], lifted[q]).astype(bf16)
        far_send[q, 0] = far[0:16]
        far_send[q, 1] = far[16:32]
        for copy in far_copies(q):
            copy.start()

    def pack(q):
        pack_next[q] = dot(lifted[q, :, 256:512], ask[0]).astype(bf16)
        pack_prev[q] = dot(lifted[q, :, 0:256], ask[1]).astype(bf16)

    lift(0)
    full_ahead.start()
    full_back.start()
    far_out(0)

    def lift_more(q, carry):
        lift(q)
        far_out(q)
        return carry

    lax.fori_loop(1, CH, lift_more, 0)
    send_a.wait()
    send_b.wait()
    ask[0] = one_hot(256, code(msg_next[16:17, :], 0))
    ask[1] = one_hot(256, code(msg_prev[16:17, :], -192))

    def answer(q, carry):
        pack(q)
        from_prev(q).start()
        from_next(q).start()
        return carry

    lax.fori_loop(1, CH, answer, 0)
    pack(0)
    ask[2] = one_hot(256, code(massx[0, 16:17, :], 0))
    ask[3] = one_hot(256, code(massx[3, 16:17, :], -192))

    def pair(ref, first, c, rows):
        return jnp.concatenate([side(ref, base, first, c) for base in rows], axis=0)

    def after(a, b):
        return jnp.where(lane < 124, pltpu.roll(a, 124, 1), pltpu.roll(b, 124, 1))

    def before(a, b):
        return jnp.where(lane < 4, pltpu.roll(a, 4, 1), pltpu.roll(b, 4, 1))

    wind_east = [msg_prev[0:8, :]] + [pair(wind, 3, c, (0, 16)) for c in range(4)]
    wind_west = [pair(wind, 0, c, (0, 16)) for c in range(4)] + [msg_next[0:8, :]]
    mass_east = [msg_prev[8:16, :]] + [pair(massx, 3, c, (0, 0)) for c in range(4)]
    mass_west = [pair(massx, 0, c, (0, 0)) for c in range(4)] + [msg_next[8:16, :]]
    west_now = [wind_west[0]] + wind_west[:4]
    mass_now = [mass_west[0]] + mass_west[:4]
    shared = []
    for i in range(5):
        mass_next = after(mass_now[i], mass_west[i])
        wind_next = after(west_now[i], wind_west[i])
        inverse = 1.0 / (mass_east[i] + mass_next)
        parts[0, i] = mass_east[i] * inverse
        parts[1, i] = mass_next * inverse
        shared.append((mass_east[i] * wind_east[i] + mass_next * wind_next) * inverse)
    for c in range(4):
        new_west = before(shared[c], shared[c + 1])
        for comp in range(2):
            wind[c, pl.ds(16 * comp + 3, 4, stride=4), :] = shared[c + 1][4 * comp : 4 * comp + 4]
            wind[c, pl.ds(16 * comp, 4, stride=4), :] = new_west[4 * comp : 4 * comp + 4]

    node = iota((16, 1), 0)

    def point(i):
        value = jnp.full(i.shape, gll[3], f32)
        for a in range(3):
            value = jnp.where(i == a, gll[a], value)
        return value

    along_point = point(jnp.bitwise_and(node, 3))
    across_point = point(jnp.right_shift(node, 2))
    for c in range(4):
        along = basis(along_point - courant * wind[c, 0:16, :])
        across = basis(across_point - courant * wind[c, 16:32, :])
        for m in range(16):
            product = across[m // 4] * along[m % 4]
            wtab[c, 16 * m : 16 * m + 16, :] = product.astype(bf16).astype(f32)

    beyond = jnp.where(lane < 4, pltpu.roll(shared[4], 4, 1), shared[0])
    along = basis(jnp.where(lane < 4, gll[0], gll[3]) - courant * beyond[0:4])
    across = basis(point(iota((4, 1), 0)) - courant * beyond[4:8])
    for m in range(16):
        product = across[m // 4] * along[m % 4]
        far_wtab[4 * m : 4 * m + 4, :] = product.astype(bf16).astype(f32)

    def gather(q, carry):
        for i, columns in enumerate(((1, 2), (0, 3))):
            block = dot(lifted[q], pick_here[i]).astype(bf16)
            for half, c in enumerate(columns):
                gath[q, c] = block[:, col(half)]
        return carry

    lax.fori_loop(0, CH, gather, 0)

    def move(q, c, block, place):
        rows = pl.ds(pl.multiple_of(q * TQ, TQ), TQ)
        values = [block[TQ * m : TQ * (m + 1), :] for m in range(16)]
        for n in range(16):
            total_n = None
            for m in range(16):
                term = wtab[c, pl.ds(16 * m + n, 1), :] * values[m]
                total_n = term if total_n is None else total_n + term
            place[n, rows, :] = total_n.astype(bf16)

    def inner(i, carry):
        q, c = i // 2, lax.rem(i, 2) + 1
        move(q, c, gath[q, c].astype(f32), moved.at[c])
        return carry

    lax.fori_loop(0, 2 * CH, inner, 0)

    full_back.wait()
    halo_next[0] = dot(full_next[...], ask[3]).astype(bf16)

    def outer_east(q, carry):
        @pl.when(q > 0)
        def _():
            from_next(q).wait()

        move(q, 3, gath[q, 3].astype(f32) + halo_next[q].astype(f32), moved.at[3])
        return carry

    lax.fori_loop(0, CH, outer_east, 0)
    def beyond_ends(q, carry):
        rows = pl.ds(pl.multiple_of(q * TQ, TQ), TQ)
        for copy in far_copies(q):
            copy.wait()
        here = jnp.where(lane < 64, pack_next[q].astype(f32), pack_prev[q].astype(f32))
        block = jnp.transpose(far_recv[q].astype(f32))
        block = jnp.where((lane < 4) | (lane >= 124), block + here, 0.0)
        values = [block[TQ * m : TQ * (m + 1), :] for m in range(16)]
        for j in range(4):
            total_j = None
            for m in range(16):
                term = far_wtab[pl.ds(4 * m + j, 1), :] * values[m]
                total_j = term if total_j is None else total_j + term
            outside[j, rows, :] = total_j.astype(bf16)
        return carry

    lax.fori_loop(0, CH, beyond_ends, 0)

    for j in range(4):
        west_raw[j] = moved[1, 4 * j]
        west = [moved[c, 4 * j].astype(f32) for c in (1, 2, 3)] + [outside[j].astype(f32)]
        joint = []
        for i, c in enumerate((1, 2, 3)):
            joint.append(
                parts[0, c + 1, j : j + 1] * moved[c, 4 * j + 3].astype(f32)
                + parts[1, c + 1, j : j + 1] * after(west[i], west[i + 1])
            )
        for i, c in enumerate((1, 2, 3)):
            first = (before(joint[i - 1], joint[i]) if i else pltpu.roll(joint[0], 4, 1)).astype(bf16)
            last = joint[i].astype(bf16)
            for half, pieces in enumerate(((first, moved[c, 4 * j + 1]), (moved[c, 4 * j + 2], last))):
                turned = jnp.concatenate(pieces, axis=0).T
                place = slice(256 * j + 128 * half, 256 * j + 128 * half + 128)
                rest[32 * i : 32 * i + 32, :, place] = turned.reshape(32, 4, 128)

    full_ahead.wait()
    halo_prev[0] = dot(full_prev[...], ask[2]).astype(bf16)

    def outer_west(q, carry):
        @pl.when(q > 0)
        def _():
            from_prev(q).wait()

        move(q, 0, gath[q, 0].astype(f32) + halo_prev[q].astype(f32), first_col)
        return carry

    lax.fori_loop(0, CH, outer_west, 0)


def share_kernel(first_col, west_raw, outside, parts, rest, o_hbm, out, patch, out_sem):
    lane = iota((1, 128), 1)

    def leave(i, src, dst):
        copy = pltpu.make_async_copy(src, dst, out_sem.at[i])
        copy.start()
        return copy

    copies = [leave(0, rest.at[1:96], o_hbm.at[33:128])]

    def after(a, b):
        return jnp.where(lane < 124, pltpu.roll(a, 124, 1), pltpu.roll(b, 124, 1))

    def before(a, b):
        return jnp.where(lane < 4, pltpu.roll(a, 4, 1), pltpu.roll(b, 4, 1))

    for j in range(4):
        west = first_col[4 * j].astype(f32)
        joint = [
            parts[0, 0, j : j + 1] * outside[j].astype(f32) + parts[1, 0, j : j + 1] * after(west, west),
            parts[0, 1, j : j + 1] * first_col[4 * j + 3].astype(f32)
            + parts[1, 1, j : j + 1] * after(west, west_raw[j].astype(f32)),
        ]
        first = before(joint[0], joint[1]).astype(bf16)
        last = joint[1].astype(bf16)
        for half, pieces in enumerate(((first, first_col[4 * j + 1]), (first_col[4 * j + 2], last))):
            turned = jnp.concatenate(pieces, axis=0).T.reshape(32, 4, 128)
            place = slice(256 * j + 128 * half, 256 * j + 128 * half + 128)
            out[:, :, place] = turned
        place = slice(256 * j, 256 * j + 128)
        moved_over = pltpu.roll(turned[31].astype(f32), 64, 1)
        patch[0, :, place] = jnp.where(lane < 64, moved_over, rest[0, :, place].astype(f32)).astype(bf16)
        place = slice(256 * j + 128, 256 * j + 256)
        patch[0, :, place] = rest[0, :, place]
    copies.append(leave(1, out, o_hbm.at[0:32]))
    copies.append(leave(2, patch, o_hbm.at[32:33]))
    for copy in copies:
        copy.wait()


def solution(mesh):
    peers_elem, peers_lev = mesh.shape["elem"], mesh.shape["lev"]

    def on_device(tracers, velocity, node_mass, source):
        elements, levels, columns = tracers.shape
        anywhere = pl.BlockSpec(memory_space=pl.ANY)
        vmem = pl.BlockSpec(memory_space=pltpu.VMEM)
        pieces = pl.pallas_call(
            functools.partial(kernel, peers_elem, peers_lev, elements * peers_elem),
            out_shape=(
                pltpu.VMEM((16, 64, 128), bf16),
                pltpu.VMEM((4, 64, 128), bf16),
                pltpu.VMEM((4, 64, 128), bf16),
                pltpu.VMEM((2, 5, 8, 128), f32),
                pltpu.VMEM((elements - 32, levels, columns), bf16),
            ),
            in_specs=[anywhere] * 4,
            out_specs=(vmem,) * 5,
            scratch_shapes=[
                pltpu.VMEM(tracers.shape, bf16),
                pltpu.VMEM(velocity.shape, f32),
                pltpu.VMEM(node_mass.shape, f32),
                pltpu.VMEM((1, elements), jnp.int32),
                pltpu.VMEM((16, 64, 512), bf16),
                pltpu.VMEM((4, 48, 128), f32),
                pltpu.VMEM((4, 24, 128), f32),
                pltpu.VMEM((24, 128), f32),
                pltpu.VMEM((24, 128), f32),
                pltpu.VMEM((24, 128), f32),
                pltpu.VMEM((24, 128), f32),
                pltpu.VMEM((CH, 16 * TQ, 128), bf16),
                pltpu.VMEM((CH, 16 * TQ, 128), bf16),
                pltpu.VMEM((CH, 16 * TQ, 512), bf16),
                pltpu.VMEM((CH, 16 * TQ, 128), bf16),
                pltpu.VMEM((CH, 16 * TQ, 128), bf16),
                pltpu.VMEM((CH, 16 * TQ, 128), bf16),
                pltpu.VMEM((CH, 16 * TQ, 128), bf16),
                pltpu.VMEM((CH, 4, 16 * TQ, 128), bf16),
                pltpu.VMEM((4, 256, 128), f32),
                pltpu.VMEM((CH, 2, 16, 16 * TQ), bf16),
                pltpu.VMEM((CH, 128, 16 * TQ), bf16),
                pltpu.VMEM((32, 512), bf16),
                pltpu.VMEM((64, 128), f32),
                pltpu.VMEM((4, 256, 128), bf16),
                pltpu.VMEM((4, 256, 128), bf16),
                pltpu.VMEM((2, 512, 256), bf16),
                pltpu.VMEM((16 * TQ, 256), bf16),
                pltpu.VMEM((16 * TQ, 256), bf16),
                pltpu.VMEM((4, 16, 64, 128), bf16),
                pltpu.SemaphoreType.DMA((4,)),
                pltpu.SemaphoreType.DMA((2, 2)),
                pltpu.SemaphoreType.DMA((CH, 2)),
                pltpu.SemaphoreType.DMA((CH, 2, 2)),
                pltpu.SemaphoreType.DMA((CH, 2, 2)),
                pltpu.SemaphoreType.DMA((2, 2)),
            ],
            compiler_params=pltpu.CompilerParams(collective_id=0, has_side_effects=True),
            name="transport",
        )(tracers, velocity, node_mass, source.reshape(1, elements))
        return pl.pallas_call(
            share_kernel,
            out_shape=jax.ShapeDtypeStruct(tracers.shape, bf16),
            in_specs=[vmem] * 5,
            out_specs=anywhere,
            scratch_shapes=[
                pltpu.VMEM((32, levels, columns), bf16),
                pltpu.VMEM((1, levels, columns), bf16),
                pltpu.SemaphoreType.DMA((3,)),
            ],
            compiler_params=pltpu.CompilerParams(vmem_limit_bytes=24 * 2**20),
            name="share",
        )(*pieces)

    placed = (P("elem", "lev", None), P(None, None, "lev", "elem"), P(None, "elem"), P("elem"))
    return jax.shard_map(
        on_device, mesh=mesh, in_specs=placed, out_specs=P("elem", "lev", None), check_vma=False
    )
```
